256 devices in a mesh: src: 32 (over y, z), dst: 8 (over x, core).
Axes of the slice: x: 4, y: 4, z: 8, core: 2. Of those that a mesh axis runs over, the one named last changes fastest.
Arguments:
- transition: bfloat16 [16384, 16384], P('src', 'dst'), may hold values from 5.4931641e-06 to 0.05
- emission: bfloat16 [8192, 16384], P('src', 'dst'), may hold values from 0.099609375 to 5
- forward: bfloat16 [3, 256, 16384], P(None, None, 'src'), may hold values from 0.25 to 4
- beta_end: bfloat16 [256, 16384], P(None, 'dst'), may hold values from 0.5 to 2
- scales: float32 [3, 256], replicated, may hold values from 0.5 to 2
- tokens: int32 [3, 256], replicated, may hold values from 0 to 8191
Outputs:
- counts: float32 [16384, 16384], P('src', 'dst')
- beta_first: float32 [256, 16384], P('dst', 'src')
The draws below stay inside these ranges and needn't reach their ends.
All inputs are finite; a program needn't handle non-finite values.
Results may differ from the reference program's by a relative error of at most 0.00076.
Values may be sent and summed in bfloat16 or wider, within the bound.
A program may use at most 64 MiB of HBM per device.

```python
import math
import jax
import jax.numpy as jnp
from jax import lax

S = 16384
V = 8192
B = 256
STEPS = 3


def draw_transition(key, part):
    first_key = jax.random.fold_in(key, 11)
    second_key = jax.random.fold_in(key, 23)
    third_key = jax.random.fold_in(key, 37)
    hits = jax.random.randint(second_key, (S, S), 0, S) < 32
    base = jnp.exp(jax.random.uniform(first_key, (S, S), jnp.float32, math.log(0.1), math.log(1.0))) / S
    spike = jnp.exp(jax.random.uniform(third_key, (S, S), jnp.float32, math.log(0.005), math.log(0.049)))
    return jnp.where(hits, spike, base).astype(jnp.bfloat16)


def place_ends(result, key, low, high):
    spot = [jax.random.randint(jax.random.fold_in(key, axis), (), 0, length) for axis, length in enumerate(result.shape)]
    main_axis = result.shape.index(max(result.shape))
    next_to = spot[:main_axis] + [(spot[main_axis] + 1) % result.shape[main_axis]] + spot[main_axis + 1:]
    return result.at[tuple(spot)].set(low).at[tuple(next_to)].set(high)


def level_of(own_key, extent, pieces, low, top_value):
    def one(position, parts):
        heights = jax.random.uniform(jax.random.fold_in(jax.random.fold_in(own_key, 6), position), (parts,), jnp.float32, low / len(pieces), top_value / len(pieces))
        return jnp.repeat(jnp.exp(heights), extent[position] // parts).reshape((-1,) + (1,) * (len(extent) - position - 1))

    loudness = one(*pieces[0])
    for cut in pieces[1:]:
        loudness = loudness * one(*cut)
    return loudness


def setup_inputs(seed: int = 0) -> dict:
    splits = jax.random.split(jax.random.key(seed), 7)
    transition = draw_transition(jax.random.fold_in(splits[6], 71), 0)
    emission = jnp.clip(jnp.exp(math.log(5.0) - 3.915937 * jax.random.uniform(splits[1], (V, S), jnp.float32) ** level_of(splits[1], (V, S), ((0, 32), (1, 8)), -0.2, 0.2)), 0.099609375, 5.0).astype(jnp.bfloat16)
    forward = jnp.clip(jnp.exp(math.log(4.0) - 2.7725887 * jax.random.uniform(splits[2], (STEPS, B, S), jnp.float32) ** level_of(splits[2], (STEPS, B, S), ((2, 32),), -0.2, 0.2)), 0.25, 4.0).astype(jnp.bfloat16)
    beta_end = jnp.clip(jnp.exp(math.log(2.0) - 1.3862944 * jax.random.uniform(splits[3], (B, S), jnp.float32) ** level_of(splits[3], (B, S), ((1, 8),), -0.2, 0.2)), 0.5, 2.0).astype(jnp.bfloat16)
    scales = jnp.clip(jnp.exp(jax.random.uniform(splits[4], (STEPS, B), jnp.float32, math.log(0.5), math.log(2.0))), 0.5, 2.0)
    tokens = place_ends(jax.random.randint(splits[5], (STEPS, B), 0, V), jax.random.fold_in(splits[5], 1), 0, V - 1).astype(jnp.int32)
    return dict(transition=transition, emission=emission, forward=forward, beta_end=beta_end, scales=scales, tokens=tokens)


def reference(transition, emission, forward, beta_end, scales, tokens):
    message = beta_end
    weights = []
    summed = jnp.zeros((B, S), jnp.float32)
    for step in range(STEPS - 1, -1, -1):
        emitted = emission[tokens[step].astype(jnp.int32)]
        weighted = (emitted.astype(jnp.float32) * message.astype(jnp.float32) / scales[step][:, None]).astype(jnp.bfloat16)
        weights.insert(0, weighted)
        summed = lax.dot_general(weighted, transition, (((1,), (1,)), ((), ())), preferred_element_type=jnp.float32)
        message = summed.astype(jnp.bfloat16)
    stacked = jnp.stack(weights, axis=0).reshape(STEPS * B, S)
    pairs = lax.dot_general(forward.reshape(STEPS * B, S), stacked, (((0,), (0,)), ((), ())), preferred_element_type=jnp.float32)
    counts = transition.astype(jnp.float32) * pairs * (32.0 / (STEPS * B))
    return counts, summed
```

```python
import jax
import jax.numpy as jnp
from jax import lax
from jax.experimental import pallas as pl
from jax.experimental.pallas import tpu as pltpu
from jax.sharding import PartitionSpec as P

MESH = pl.DeviceIdType.MESH
NX, NY, NZ, NC = 4, 4, 8, 2
B = 256
STEPS = 3
BF = jnp.bfloat16
F32 = jnp.float32


def dev(x, y, z, c):
    return (y * NZ + z, x * NC + c)


def kernel(
    trans, emis, forw, beta, scales, tokens,
    counts, first,
    tv, ev, fv, bv, ft, sc, tc,
    x2, rz2, x10, rz10, em_s, em,
    w, own, pb, pr, qb, orx, fp, fr, fq, fx, cb,
    l_sem, out_sem,
    e_s, e_r, z2_s, z2_r, zw_s, zw_r, z10_s, z10_r, pm_s, pm_r,
    y_s, y_r, pp_s, pp_r, o_s, o_r, zz_s, zz_r, fp_s, fp_r, fx_s, fx_r,
):
    s = lax.axis_index("src")
    d = lax.axis_index("dst")
    y, z = s // NZ, s % NZ
    x, c = d // NC, d % NC
    sib = 1 - c
    words = emis.shape[0]
    cols = emis.shape[1]
    blk = cols // 4
    rows = trans.shape[0]
    yo = pl.multiple_of(y * blk, blk)
    oc = z // 4
    q = z % 4
    qo = pl.multiple_of(q * blk, blk)
    is_owner = c == oc

    def zp(i):
        return lax.rem(z + i, NZ)

    def yp(i):
        return lax.rem(y + i, NY)

    def xp(i):
        return lax.rem(x + i, NX)

    barrier = pltpu.get_barrier_semaphore()
    peers = (
        [dev(x, y, z, sib)]
        + [dev(x, yp(i), z, c) for i in range(1, NY)]
        + [dev(x, y, zp(i), c) for i in range(1, NZ)]
        + [dev(xp(i), y, z, c) for i in range(1, NX)]
    )
    for p in peers:
        pl.semaphore_signal(barrier, inc=1, device_id=p, device_id_type=MESH)

    loads = [
        pltpu.make_async_copy(emis.at[:, pl.ds(yo, blk)], ev.at[y], l_sem.at[0]),
        pltpu.make_async_copy(
            beta.at[pl.ds(pl.multiple_of(z * 32, 32), 32), pl.ds(yo, blk)], bv, l_sem.at[1]
        ),
        pltpu.make_async_copy(trans, tv, l_sem.at[2]),
        pltpu.make_async_copy(forw, fv, l_sem.at[3]),
    ]
    for cp in loads:
        cp.start()

    pl.semaphore_wait(barrier, len(peers))

    sends = []

    def remote(src, dst, ss, rs, to):
        return pltpu.make_async_remote_copy(
            src_ref=src, dst_ref=dst, send_sem=ss, recv_sem=rs, device_id=to, device_id_type=MESH
        )

    def send(cp, cond=None):
        if cond is None:
            cp.start()
        else:
            pl.when(cond)(cp.start)
        sends.append((cond, cp))

    def arrive(cp, cond=None):
        if cond is None:
            cp.wait_recv()
        else:
            pl.when(cond)(cp.wait_recv)

    here = dev(x, y, z, sib)

    def landing(dst, rs):
        return remote(dst, dst, rs, rs, here)

    for i in (2, 1, 3):
        yt = yp(i)
        send(
            remote(
                emis.at[:, pl.ds(pl.multiple_of(yt * blk, blk), blk)],
                ev.at[y], e_s.at[i - 1], e_r.at[i - 1], dev(x, yt, z, c),
            )
        )

    eye = lax.broadcasted_iota(jnp.int32, (B, B), 0) == lax.broadcasted_iota(jnp.int32, (B, B), 1)
    for k in range(STEPS):
        for src, dst in ((scales[k : k + 1, :], sc), (tokens[k : k + 1, :].astype(F32), tc)):
            col = jnp.sum(jnp.where(eye, jnp.broadcast_to(src, (B, B)), 0.0), axis=1, keepdims=True)
            dst[k] = jnp.broadcast_to(col, (B, 128)).reshape(8, 32, 128)

    loads[3].wait()
    for k in range(STEPS):
        ft[:, k * B : (k + 1) * B] = fv[k].astype(F32).T.astype(BF)
    loads[2].wait()
    loads[1].wait()

    def lookup(k):
        tok = tc[k].reshape(B, 128)
        acc = jnp.zeros((B, blk), F32)
        for j in range(NY):
            base = ((j * NZ + z) * words).astype(F32)
            parts = []
            for t in range(words // 128):
                lane = lax.broadcasted_iota(jnp.int32, (B, 128), 1).astype(F32) + (base + 128.0 * t)
                parts.append(jnp.where(tok == lane, 1.0, 0.0).astype(BF))
            hot = jnp.concatenate(parts, axis=1)
            acc = acc + jnp.dot(hot, ev[j], preferred_element_type=F32)
        return acc.astype(BF).reshape(8, 32, blk)

    loads[0].wait()
    for i in (1, 3, 2):
        arrive(landing(ev.at[yp(NY - i)], e_r.at[i - 1]))
    x2[...] = lookup(2)
    for i in (4, 3, 5, 2, 6, 1, 7):
        send(remote(x2.at[zp(i)], rz2.at[i - 1], z2_s.at[i - 1], z2_r.at[i - 1], dev(x, y, zp(i), c)))
    for kk in range(2):
        x10[:, kk] = lookup(kk)

    tot = x2[z].astype(F32)
    for i in (1, 7, 2, 6, 3, 5, 4):
        arrive(landing(rz2.at[i - 1], z2_r.at[i - 1]))
        tot = tot + rz2[i - 1].astype(F32)

    def scaled(value, k, g):
        den = sc[k, g]
        return value / jnp.concatenate([den] * (blk // 128), axis=1)

    w[2, z // 2, z % 2, :, pl.ds(yo, blk)] = scaled(tot * bv[...].astype(F32), 2, z).astype(BF)
    mine = w.at[2, z // 2, z % 2, :, pl.ds(yo, blk)]
    for i in (4, 3, 5, 2, 6, 1, 7):
        send(remote(mine, mine, zw_s.at[i - 1], zw_r.at[i - 1], dev(x, y, zp(i), c)))
    for i in (1, 7, 2, 6, 3, 5, 4):
        zt = zp(NZ - i)
        arrive(landing(w.at[2, zt // 2, zt % 2, :, pl.ds(yo, blk)], zw_r.at[i - 1]))
    for h in range(2):
        part = w.at[2, :, h, :, pl.ds(yo, blk)]
        for i in (2, 1, 3):
            send(remote(part, part, y_s.at[2, h, i - 1], y_r.at[2, h, i - 1], dev(x, yp(i), z, c)))

    for i in (4, 3, 5, 2, 6, 1, 7):
        send(
            remote(x10.at[zp(i)], rz10.at[i - 1], z10_s.at[i - 1], z10_r.at[i - 1], dev(x, y, zp(i), c))
        )

    def wait_rows(k, h):
        for i in (1, 3, 2):
            yt = yp(NY - i)
            if k == 2:
                dst = w.at[2, :, h, :, pl.ds(pl.multiple_of(yt * blk, blk), blk)]
            else:
                dst = w.at[k, yt, h]
            arrive(landing(dst, y_r.at[k, h, i - 1]))

    def product(k, h, n):
        return lax.dot_general(
            w[k, :, h].reshape(B // 2, cols), tv[n * 256 : (n + 1) * 256, :],
            (((1,), (1,)), ((), ())), preferred_element_type=F32,
        )

    for k in (1, 0):
        for h in range(2):
            wait_rows(k + 1, h)
            for n in range(rows // 256):
                res = product(k + 1, h, n).reshape(4, 2, 16, 256)
                for cc in range(2):
                    own[k, h, cc, :, :, n * 256 : (n + 1) * 256] = res[:, cc]
                    pb[k, h, cc, :, :, n * 256 : (n + 1) * 256] = res[:, cc].astype(BF)
            send(
                remote(pb.at[k, h, sib], pr.at[k, h], pp_s.at[k, h], pp_r.at[k, h], dev(x, y, z, sib))
            )
        for h in range(2):
            arrive(landing(pr.at[k, h], pp_r.at[k, h]))
            qb[k, h] = (own[k, h, c] + pr[k, h].astype(F32)).astype(BF)
            for r in range(NY):
                self_r = (x == y) & (y == r) & is_owner
                send(
                    remote(
                        qb.at[k, h, r], orx.at[k, h, x, c], o_s.at[k, h, r], o_r.at[k, h, x * 2 + c],
                        dev(y, r, z, oc),
                    ),
                    jnp.logical_not(self_r),
                )

                @pl.when(self_r)
                def _():
                    orx[k, h, x, c] = qb[k, h, r]

        if k == 1:
            for kk in range(2):
                acc = x10[z, kk].astype(F32)
                for i in (1, 7, 2, 6, 3, 5, 4):
                    if kk == 0:
                        arrive(landing(rz10.at[i - 1], z10_r.at[i - 1]))
                    acc = acc + rz10[i - 1, kk].astype(F32)
                em_s[kk] = acc.astype(BF)
            pm_self = (y == z // 2) & (z == 4 * c + y)
            send(
                remote(em_s, em.at[z % 2], pm_s.at[0], pm_r.at[z % 2], dev(x, z // 2, 4 * c + y, c)),
                jnp.logical_not(pm_self),
            )

            @pl.when(pm_self)
            def _():
                em[z % 2] = em_s[...]

            for h in range(2):
                from_self = (y == q) & (z == 2 * y + h)
                arrive(landing(em.at[h], pm_r.at[h]), is_owner & jnp.logical_not(from_self))

        for h in range(2):
            for j in range(8):
                from_self = (x == y) & (x * 2 + c == j)
                arrive(
                    landing(orx.at[k, h, j // 2, j % 2], o_r.at[k, h, j]),
                    is_owner & jnp.logical_not(from_self),
                )

            @pl.when(is_owner)
            def _():
                halves = []
                for cc in range(2):
                    acc = orx[k, h, 0, cc].astype(F32)
                    for xx in range(1, NX):
                        acc = acc + orx[k, h, xx, cc].astype(F32)
                    halves.append(acc)
                msg = jnp.concatenate(halves, axis=0).astype(BF).astype(F32)
                w[k, y, h, :, pl.ds(qo, blk)] = scaled(
                    em[h, k].astype(F32) * msg, k, 2 * y + h
                ).astype(BF)

            tile = w.at[k, y, h, :, pl.ds(qo, blk)]
            for i in (4, 3, 5, 2, 6, 1, 7):
                send(
                    remote(tile, tile, zz_s.at[k, h, i - 1], zz_r.at[k, h, q], dev(x, y, zp(i), c)),
                    is_owner,
                )
        for h in range(2):
            for j in range(4):
                arrive(
                    landing(w.at[k, y, h, :, j * blk : (j + 1) * blk], zz_r.at[k, h, j]),
                    z != 4 * c + j,
                )
            part = w.at[k, y, h]
            for i in (2, 1, 3):
                send(remote(part, part, y_s.at[k, h, i - 1], y_r.at[k, h, i - 1], dev(x, yp(i), z, c)))

    for h in range(2):
        wait_rows(0, h)
        for n in range(rows // 256):
            fp[h, :, :, n * 256 : (n + 1) * 256] = product(0, h, n).reshape(4, 32, 256)
    send(remote(fp.at[sib], fr, fp_s.at[0], fp_r.at[0], dev(x, y, z, sib)))

    def count_block(n):
        lo = n * 256
        acc = jnp.dot(
            ft[...], w[:, :, :, :, lo : lo + 256].reshape(STEPS * B, 256), preferred_element_type=F32
        )
        cb[:, lo : lo + 256] = tv[:, lo : lo + 256].astype(F32) * acc * (32.0 / (STEPS * B))
        cp = pltpu.make_async_copy(
            cb.at[:, lo : lo + 256], counts.at[:, lo : lo + 256], out_sem.at[n]
        )
        cp.start()
        return cp

    outs = [count_block(n) for n in range(2)]
    arrive(landing(fr, fp_r.at[0]))
    fq[...] = fp[c] + fr[...]
    for i in (2, 1, 3):
        send(remote(fq.at[xp(i)], fx.at[i - 1], fx_s.at[i - 1], fx_r.at[i - 1], dev(xp(i), y, z, c)))
    outs += [count_block(n) for n in range(2, cols // 256)]
    tot = fq[x]
    for i in (1, 3, 2):
        arrive(landing(fx.at[i - 1], fx_r.at[i - 1]))
        tot = tot + fx[i - 1]
    first[...] = tot
    for cond, cp in sends:
        if cond is None:
            cp.wait_send()
        else:
            pl.when(cond)(cp.wait_send)
    for cp in outs:
        cp.wait()


def per_device(transition, emission, forward, beta_end, scales, tokens):
    rows, cols = transition.shape
    blk = cols // 4
    dma = pltpu.SemaphoreType.DMA
    vm = pltpu.VMEM
    hbm = pl.BlockSpec(memory_space=pl.ANY)
    vmem = pl.BlockSpec(memory_space=pltpu.VMEM)
    return pl.pallas_call(
        kernel,
        out_shape=(
            jax.ShapeDtypeStruct((rows, cols), F32),
            jax.ShapeDtypeStruct((B // 8, rows), F32),
        ),
        in_specs=[hbm, hbm, hbm, hbm, vmem, vmem],
        out_specs=(hbm, vmem),
        scratch_shapes=[
            vm((rows, cols), BF),
            vm((NY, emission.shape[0], blk), BF),
            vm((STEPS, B, rows), BF),
            vm((32, blk), BF),
            vm((rows, STEPS * B), BF),
            vm((STEPS, 8, 32, 128), F32),
            vm((STEPS, 8, 32, 128), F32),
            vm((8, 32, blk), BF),
            vm((7, 32, blk), BF),
            vm((8, 2, 32, blk), BF),
            vm((7, 2, 32, blk), BF),
            vm((2, 32, blk), BF),
            vm((2, 2, 32, blk), BF),
            vm((STEPS, 4, 2, 32, cols), BF),
            vm((2, 2, 2, 4, 16, rows), F32),
            vm((2, 2, 2, 4, 16, rows), BF),
            vm((2, 2, 4, 16, rows), BF),
            vm((2, 2, 4, 16, rows), BF),
            vm((2, 2, NX, NC, 16, rows), BF),
            vm((2, 4, 32, rows), F32),
            vm((4, 32, rows), F32),
            vm((4, 32, rows), F32),
            vm((3, 32, rows), F32),
            vm((rows, cols), F32),
            dma((4,)),
            dma((8,)),
            dma((3,)), dma((3,)),
            dma((7,)), dma((7,)),
            dma((7,)), dma((7,)),
            dma((7,)), dma((7,)),
            dma((1,)), dma((2,)),
            dma((3, 2, 3)), dma((3, 2, 3)),
            dma((2, 2)), dma((2, 2)),
            dma((2, 2, 4)), dma((2, 2, 8)),
            dma((2, 2, 7)), dma((2, 2, 4)),
            dma((1,)), dma((1,)),
            dma((3,)), dma((3,)),
        ],
        compiler_params=pltpu.CompilerParams(
            collective_id=0, has_side_effects=True, vmem_limit_bytes=48 * 1024 * 1024
        ),
        name="window",
    )(transition, emission, forward, beta_end, scales, tokens)


def solution(mesh):
    in_specs = (P("src", "dst"), P("src", "dst"), P(None, None, "src"), P(None, "dst"), P(), P())
    out_specs = (P("src", "dst"), P("dst", "src"))
    return jax.shard_map(
        per_device, mesh=mesh, in_specs=in_specs, out_specs=out_specs, check_vma=False
    )
```

```python
import jax
import jax.numpy as jnp
from jax import lax
from jax.experimental import pallas as pl
from jax.experimental.pallas import tpu as pltpu
from jax.sharding import PartitionSpec as P

MESH = pl.DeviceIdType.MESH
NX, NY, NZ, NC = 4, 4, 8, 2
B = 256
STEPS = 3
NT = 4
BF = jnp.bfloat16
F32 = jnp.float32
FAR = (4, 3, 5, 2, 6, 1, 7)
NEAR = (1, 7, 2, 6, 3, 5, 4)


def dev(x, y, z, c):
    return (y * NZ + z, x * NC + c)


def kernel(
    trans, emis, forw, beta, scales_in, tokens_in,
    counts, first,
    scales, tokens, tv, tt, ev, fv, bv, ft, sc, tc, hot,
    x2, rz2, x10, rz10, em_s, em,
    w, own, pb, pr, qb, orx, fp, fx,
    l_sem, rdy,
    e_s, e_r, z2_s, z2_r, zw_s, zw_r, z10_s, z10_r, pm_s, pm_r,
    y_s, y_r, pp_s, pp_r, o_s, o_r, zz_s, zz_r, fx_s, fx_r,
):
    s = lax.axis_index("src")
    d = lax.axis_index("dst")
    y, z = s // NZ, s % NZ
    x, c = d // NC, d % NC
    sib = 1 - c
    words = emis.shape[0]
    cols = emis.shape[1]
    blk = cols // 4
    hb = blk // 2
    rows = trans.shape[0]
    yo = pl.multiple_of(y * blk, blk)
    oc = z // 4
    q = z % 4
    qo = pl.multiple_of(q * blk, blk)
    is_owner = c == oc

    def zp(i):
        return lax.rem(z + i, NZ)

    def yp(i):
        return lax.rem(y + i, NY)

    def xp(i):
        return lax.rem(x + i, NX)

    barrier = pltpu.get_barrier_semaphore()
    z_near = [dev(x, y, zp(i), c) for i in (1, NZ - 1)]
    x_near = [dev(xp(i), y, z, c) for i in (1, NX - 1)]
    peers = [dev(x, y, z, sib)] + [dev(x, yp(i), z, c) for i in range(1, NY)] + z_near + x_near

    def greet(sem, to):
        for p in to:
            pl.semaphore_signal(sem, inc=1, device_id=p, device_id_type=MESH)

    greet(barrier, peers)
    loads = [
        pltpu.make_async_copy(emis.at[:, pl.ds(yo, hb)], ev.at[0, y], l_sem.at[0]),
        pltpu.make_async_copy(
            emis.at[:, pl.ds(pl.multiple_of(y * blk + hb, hb), hb)], ev.at[1, y], l_sem.at[1]
        ),
        pltpu.make_async_copy(
            beta.at[pl.ds(pl.multiple_of(z * 32, 32), 32), pl.ds(yo, blk)], bv, l_sem.at[2]
        ),
        pltpu.make_async_copy(trans, tv, l_sem.at[3]),
        pltpu.make_async_copy(forw, fv, l_sem.at[4]),
        pltpu.make_async_copy(scales_in, scales, l_sem.at[5]),
        pltpu.make_async_copy(tokens_in, tokens, l_sem.at[6]),
    ]
    for cp in loads:
        cp.start()
    pl.semaphore_wait(barrier, len(peers))

    sends = []

    def remote(src, dst, ss, rs, to):
        return pltpu.make_async_remote_copy(
            src_ref=src, dst_ref=dst, send_sem=ss, recv_sem=rs, device_id=to, device_id_type=MESH
        )

    def send(cp, cond=None):
        if cond is None:
            cp.start()
        else:
            pl.when(cond)(cp.start)
        sends.append((cond, cp))

    here = dev(x, y, z, sib)

    def arrive(dst, rs, cond=None):
        cp = remote(dst, dst, rs, rs, here)
        if cond is None:
            cp.wait_recv()
        else:
            pl.when(cond)(cp.wait_recv)

    for h in range(2):
        for i in (2, 1, 3):
            yt = yp(i)
            send(
                remote(
                    emis.at[:, pl.ds(pl.multiple_of(yt * blk + h * hb, hb), hb)],
                    ev.at[h, y], e_s.at[h, i - 1], e_r.at[h, i - 1], dev(x, yt, z, c),
                )
            )

    for cp in loads[2:]:
        cp.wait()
    eye = lax.broadcasted_iota(jnp.int32, (B, B), 0) == lax.broadcasted_iota(jnp.int32, (B, B), 1)
    for k in (2, 1, 0):
        for src, dst in ((tokens[k : k + 1, :].astype(F32), tc), (scales[k : k + 1, :], sc)):
            col = jnp.sum(jnp.where(eye, jnp.broadcast_to(src, (B, B)), 0.0), axis=1, keepdims=True)
            dst[k] = jnp.broadcast_to(col, (B, 128)).reshape(16, 16, 128)
        tok = tc[k].reshape(B, 128)
        for j in range(NY):
            base = ((j * NZ + z) * words).astype(F32)
            for t in range(words // 128):
                lane = lax.broadcasted_iota(jnp.int32, (B, 128), 1).astype(F32) + (base + 128.0 * t)
                at = j * words + t * 128
                hot[k, :, at : at + 128] = jnp.where(tok == lane, 1.0, 0.0).astype(BF)
    for k in range(STEPS):
        ft[:, k * B : (k + 1) * B] = fv[k].astype(F32).T.astype(BF)

    greet(rdy.at[3], x_near)
    for j in range(3):
        greet(rdy.at[j], z_near)
        pl.semaphore_wait(rdy.at[j], 2)
    pl.semaphore_wait(rdy.at[3], 2)

    def lookup(k, h):
        return jnp.dot(
            hot[k], ev[h].reshape(NY * words, hb), preferred_element_type=F32
        ).astype(BF).reshape(8, 32, hb)

    for h in range(2):
        loads[h].wait()
        for i in (1, 3, 2):
            arrive(ev.at[h, yp(NY - i)], e_r.at[h, i - 1])
        x2[h] = lookup(2, h)
        for i in FAR:
            send(
                remote(
                    x2.at[h, zp(i)], rz2.at[h, i - 1], z2_s.at[h, i - 1], z2_r.at[h, i - 1],
                    dev(x, y, zp(i), c),
                )
            )
        part = pl.multiple_of((sib if h == 0 else c) * (rows // 2), rows // 2)
        for lo in range(0, cols, 512):
            tt[h, lo : lo + 512, :] = tv[pl.ds(part, rows // 2), lo : lo + 512].astype(F32).T.astype(BF)

    for kk in (1, 0):
        for h in range(2):
            x10[kk, :, :, h * hb : (h + 1) * hb] = lookup(kk, h)

    def scaled(value, k, g):
        den = sc[k, g]
        return value / jnp.concatenate([den] * (value.shape[-1] // 128), axis=1)

    for h in range(2):
        tot = x2[h, z].astype(F32)
        for i in NEAR:
            arrive(rz2.at[h, i - 1], z2_r.at[h, i - 1])
            tot = tot + rz2[h, i - 1].astype(F32)
        tot = tot * bv[:, h * hb : (h + 1) * hb].astype(F32)
        ho = pl.ds(pl.multiple_of(y * blk + h * hb, hb), hb)
        for u in range(2):
            w[2, z // 2, 2 * (z % 2) + u, :, ho] = scaled(
                tot[u * 16 : (u + 1) * 16], 2, 2 * z + u
            ).astype(BF)
        mine = w.at[2, z // 2, pl.ds(2 * (z % 2), 2), :, ho]
        for i in FAR:
            send(
                remote(mine, mine, zw_s.at[h, i - 1], zw_r.at[h, i - 1], dev(x, y, zp(i), c))
            )

    def spread(kk):
        for i in FAR:
            send(
                remote(
                    x10.at[kk, zp(i)], rz10.at[kk, i - 1], z10_s.at[kk, i - 1], z10_r.at[kk, i - 1],
                    dev(x, y, zp(i), c),
                )
            )

    spread(1)
    for h in range(2):
        ho = pl.ds(pl.multiple_of(y * blk + h * hb, hb), hb)
        for i in NEAR:
            zt = zp(NZ - i)
            arrive(w.at[2, zt // 2, pl.ds(2 * (zt % 2), 2), :, ho], zw_r.at[h, i - 1])
    def y_part(k, t, yt):
        if k == 2:
            return w.at[2, :, t, :, pl.ds(pl.multiple_of(yt * blk, blk), blk)]
        return w.at[k, yt, t]

    def y_send(k, t):
        part = y_part(k, t, y)
        for i in (2, 1, 3):
            send(remote(part, part, y_s.at[k, t, i - 1], y_r.at[k, t, i - 1], dev(x, yp(i), z, c)))

    for t in range(NT):
        y_send(2, t)
    spread(0)

    def wait_rows(k, t):
        for i in (1, 3, 2):
            arrive(y_part(k, t, yp(NY - i)), y_r.at[k, t, i - 1])

    def product(k, t, j):
        return jnp.dot(
            w[k, :, t].reshape(B // NT, cols), tt[j], preferred_element_type=F32
        ).reshape(4, 16, rows // 2)

    def rows_of(k, t):
        wait_rows(k + 1, t)
        pb[k, t] = product(k + 1, t, 0).astype(BF)
        send(remote(pb.at[k, t], pr.at[k, t], pp_s.at[k, t], pp_r.at[k, t], dev(x, y, z, sib)))
        own[k, t] = product(k + 1, t, 1)
        arrive(pr.at[k, t], pp_r.at[k, t])
        qb[k, t] = (own[k, t] + pr[k, t].astype(F32)).astype(BF)
        for r in range(NY):
            self_r = (x == y) & (y == r) & is_owner
            send(
                remote(
                    qb.at[k, t, r], orx.at[k, t, x, c], o_s.at[k, t, r], o_r.at[k, t, x * 2 + c],
                    dev(y, r, z, oc),
                ),
                jnp.logical_not(self_r),
            )

            @pl.when(self_r)
            def _():
                orx[k, t, x, c] = qb[k, t, r]

    pm_self = (y == z // 2) & (z == 4 * c + y)

    def tiles(kk):
        acc = x10[kk, z].astype(F32)
        for i in NEAR:
            arrive(rz10.at[kk, i - 1], z10_r.at[kk, i - 1])
            acc = acc + rz10[kk, i - 1].astype(F32)
        em_s[kk] = acc.astype(BF)
        send(
            remote(
                em_s.at[kk], em.at[kk, z % 2], pm_s.at[kk], pm_r.at[kk, z % 2],
                dev(x, z // 2, 4 * c + y, c),
            ),
            jnp.logical_not(pm_self),
        )

        @pl.when(pm_self)
        def _():
            em[kk, z % 2] = em_s[kk]

    def tiles_done(kk):
        for h in range(2):
            from_self = (y == q) & (z == 2 * y + h)
            arrive(em.at[kk, h], pm_r.at[kk, h], is_owner & jnp.logical_not(from_self))

    def owner(k, t):
        for j in range(8):
            from_self = (x == y) & (x * 2 + c == j)
            arrive(
                orx.at[k, t, j // 2, j % 2], o_r.at[k, t, j],
                is_owner & jnp.logical_not(from_self),
            )

        @pl.when(is_owner)
        def _():
            halves = []
            for cc in range(2):
                acc = orx[k, t, 0, cc].astype(F32)
                for xx in range(1, NX):
                    acc = acc + orx[k, t, xx, cc].astype(F32)
                halves.append(acc)
            msg = jnp.concatenate(halves, axis=1).astype(BF).astype(F32)
            lo = 16 * (t % 2)
            w[k, y, t, :, pl.ds(qo, blk)] = scaled(
                em[k, t // 2, lo : lo + 16].astype(F32) * msg, k, 4 * y + t
            ).astype(BF)

        tile = w.at[k, y, t, :, pl.ds(qo, blk)]
        for i in FAR:
            send(
                remote(tile, tile, zz_s.at[k, t, i - 1], zz_r.at[k, t, q], dev(x, y, zp(i), c)),
                is_owner,
            )

    def column(k, t):
        for j in range(4):
            arrive(w.at[k, y, t, :, j * blk : (j + 1) * blk], zz_r.at[k, t, j], z != 4 * c + j)
        y_send(k, t)

    def last(t):
        wait_rows(0, t)
        for j, half in ((0, sib), (1, c)):
            fp[t, :, :, pl.ds(pl.multiple_of(half * (rows // 2), rows // 2), rows // 2)] = product(
                0, t, j
            )
        to = t // 2
        u = t % 2
        for i in (2, 1, 3, 0):
            send(
                remote(
                    fp.at[t, xp(i)], fx.at[u, i, c], fx_s.at[t, i], fx_r.at[u, i, c],
                    dev(xp(i), y, z, to),
                ),
                c != to if i == 0 else None,
            )

    rows_of(1, 0)
    rows_of(1, 1)
    tiles(1)
    rows_of(1, 2)
    tiles_done(1)
    owner(1, 0)
    rows_of(1, 3)
    owner(1, 1)
    owner(1, 2)
    column(1, 0)
    owner(1, 3)
    column(1, 1)
    tiles(0)
    column(1, 2)
    rows_of(0, 0)
    column(1, 3)
    rows_of(0, 1)
    rows_of(0, 2)
    tiles_done(0)
    owner(0, 0)
    rows_of(0, 3)
    owner(0, 1)
    owner(0, 2)
    column(0, 0)
    owner(0, 3)
    column(0, 1)
    column(0, 2)
    last(0)
    column(0, 3)
    last(1)
    last(2)
    last(3)

    def count_block(n):
        lo = n * 256
        acc = jnp.dot(
            ft[...], w[:, :, :, :, lo : lo + 256].reshape(STEPS * B, 256), preferred_element_type=F32
        )
        counts[:, lo : lo + 256] = tv[:, lo : lo + 256].astype(F32) * acc * (32.0 / (STEPS * B))

    for n in range(cols // 256):
        count_block(n)
    for u in range(2):
        tot = fp[2 * c + u, x]
        for i, core in [(0, sib)] + [(i, j) for i in (1, 3, 2) for j in range(2)]:
            arrive(fx.at[u, i, core], fx_r.at[u, i, core])
            tot = tot + fx[u, i, core]
        first[u * 16 : (u + 1) * 16] = tot
    for cond, cp in sends:
        if cond is None:
            cp.wait_send()
        else:
            pl.when(cond)(cp.wait_send)


def per_device(*args):
    transition, emission = args[:2]
    rows, cols = transition.shape
    blk = cols // 4
    words = emission.shape[0]
    dma = pltpu.SemaphoreType.DMA
    vm = pltpu.VMEM
    hbm = pl.BlockSpec(memory_space=pltpu.HBM)
    vmem = pl.BlockSpec(memory_space=pltpu.VMEM)
    return pl.pallas_call(
        kernel,
        out_shape=(
            jax.ShapeDtypeStruct((rows, cols), F32),
            jax.ShapeDtypeStruct((B // 8, rows), F32),
        ),
        in_specs=[hbm] * 6,
        out_specs=(vmem, vmem),
        scratch_shapes=[
            vm((STEPS, B), F32),
            vm((STEPS, B), jnp.int32),
            vm((rows, cols), BF),
            vm((2, cols, rows // 2), BF),
            vm((2, NY, words, blk // 2), BF),
            vm((STEPS, B, rows), BF),
            vm((32, blk), BF),
            vm((rows, STEPS * B), BF),
            vm((STEPS, 16, 16, 128), F32),
            vm((STEPS, 16, 16, 128), F32),
            vm((STEPS, B, NY * words), BF),
            vm((2, 8, 32, blk // 2), BF),
            vm((2, 7, 32, blk // 2), BF),
            vm((2, 8, 32, blk), BF),
            vm((2, 7, 32, blk), BF),
            vm((2, 32, blk), BF),
            vm((2, 2, 32, blk), BF),
            vm((STEPS, 4, NT, 16, cols), BF),
            vm((2, NT, 4, 16, rows // 2), F32),
            vm((2, NT, 4, 16, rows // 2), BF),
            vm((2, NT, 4, 16, rows // 2), BF),
            vm((2, NT, 4, 16, rows // 2), BF),
            vm((2, NT, NX, NC, 16, rows // 2), BF),
            vm((NT, 4, 16, rows), F32),
            vm((2, NX, NC, 16, rows), F32),
            dma((7,)),
            pltpu.SemaphoreType.REGULAR((4,)),
            dma((2, 3)), dma((2, 3)),
            dma((2, 7)), dma((2, 7)),
            dma((2, 7)), dma((2, 7)),
            dma((2, 7)), dma((2, 7)),
            dma((2,)), dma((2, 2)),
            dma((3, NT, 3)), dma((3, NT, 3)),
            dma((2, NT)), dma((2, NT)),
            dma((2, NT, 4)), dma((2, NT, 8)),
            dma((2, NT, 7)), dma((2, NT, 4)),
            dma((NT, NX)), dma((2, NX, NC)),
        ],
        compiler_params=pltpu.CompilerParams(
            collective_id=0, has_side_effects=True, vmem_limit_bytes=30 * 1024 * 1024
        ),
        name="window",
    )(*(pltpu.with_memory_space_constraint(a, pltpu.HBM) for a in args))


def solution(mesh):
    in_specs = (P("src", "dst"), P("src", "dst"), P(None, None, "src"), P(None, "dst"), P(), P())
    out_specs = (P("src", "dst"), P("dst", "src"))
    return jax.shard_map(
        per_device, mesh=mesh, in_specs=in_specs, out_specs=out_specs, check_vma=False
    )
```

```python
import jax
import jax.numpy as jnp
from jax import lax
from jax.experimental import pallas as pl
from jax.experimental.pallas import tpu as pltpu
from jax.sharding import PartitionSpec as P

MESH = pl.DeviceIdType.MESH
NX, NY, NZ, NC = 4, 4, 8, 2
B = 256
STEPS = 3
NT = 4
BF = jnp.bfloat16
F32 = jnp.float32
FAR = (4, 3, 5, 2, 6, 1, 7)
NEAR = (1, 7, 2, 6, 3, 5, 4)


def dev(x, y, z, c):
    return (y * NZ + z, x * NC + c)


def kernel(
    trans, emis, forw, beta, scales_in, tokens_in,
    counts, first,
    scales, tokens, tv, tt, ev, fv, bv, ft, sc, tc, hot,
    x2, rz2, x10, rz10, em_s, em,
    w, own, pb, pr, qb, orx, fp, fx,
    l_sem, rdy,
    e_s, e_r, z2_s, z2_r, zw_s, zw_r, z10_s, z10_r, pm_s, pm_r,
    ya_s, ya_r, y_s, y_r, pp_s, pp_r, o_s, o_r, zz_s, zz_r, fx_s, fx_r,
):
    s = lax.axis_index("src")
    d = lax.axis_index("dst")
    y, z = s // NZ, s % NZ
    x, c = d // NC, d % NC
    sib = 1 - c
    words = emis.shape[0]
    cols = emis.shape[1]
    blk = cols // 4
    hb = blk // 2
    rows = trans.shape[0]
    yo = pl.multiple_of(y * blk, blk)
    oc = z // 4
    q = z % 4
    qo = pl.multiple_of(q * blk, blk)
    is_owner = c == oc

    def zp(i):
        return lax.rem(z + i, NZ)

    def yp(i):
        return lax.rem(y + i, NY)

    def xp(i):
        return lax.rem(x + i, NX)

    barrier = pltpu.get_barrier_semaphore()
    z_near = [dev(x, y, zp(i), c) for i in (1, NZ - 1)]
    x_near = [dev(xp(i), y, z, c) for i in (1, NX - 1)]
    peers = [dev(x, y, z, sib)] + [dev(x, yp(i), z, c) for i in range(1, NY)] + z_near + x_near

    def greet(sem, to):
        for p in to:
            pl.semaphore_signal(sem, inc=1, device_id=p, device_id_type=MESH)

    greet(barrier, peers)
    loads = [
        pltpu.make_async_copy(emis.at[:, pl.ds(yo, hb)], ev.at[0, y], l_sem.at[0]),
        pltpu.make_async_copy(
            emis.at[:, pl.ds(pl.multiple_of(y * blk + hb, hb), hb)], ev.at[1, y], l_sem.at[1]
        ),
        pltpu.make_async_copy(
            beta.at[pl.ds(pl.multiple_of(z * 32, 32), 32), pl.ds(yo, blk)], bv, l_sem.at[2]
        ),
        pltpu.make_async_copy(trans, tv, l_sem.at[3]),
        pltpu.make_async_copy(forw, fv, l_sem.at[4]),
        pltpu.make_async_copy(scales_in, scales, l_sem.at[5]),
        pltpu.make_async_copy(tokens_in, tokens, l_sem.at[6]),
    ]
    for cp in loads:
        cp.start()
    pl.semaphore_wait(barrier, len(peers))

    sent = []

    def send(src, dst, ss, rs, to, cond=None):
        cp = pltpu.make_async_remote_copy(
            src_ref=src, dst_ref=dst, send_sem=ss, recv_sem=rs, device_id=to, device_id_type=MESH
        )
        if cond is None:
            cp.start()
        else:
            pl.when(cond)(cp.start)

    def sent_all(size, sem, cond=None):
        sent.append((cond, size, sem))

    here = dev(x, y, z, sib)

    def whole(size, sem):
        return pltpu.make_async_remote_copy(
            src_ref=size, dst_ref=size, send_sem=sem, recv_sem=sem,
            device_id=here, device_id_type=MESH,
        )

    def arrive(size, sem, cond=None):
        wait = whole(size, sem).wait_recv
        if cond is None:
            wait()
        else:
            pl.when(cond)(wait)

    for h in range(2):
        for i in (2, 1, 3):
            yt = yp(i)
            send(
                emis.at[:, pl.ds(pl.multiple_of(yt * blk + h * hb, hb), hb)],
                ev.at[h, y], e_s.at[h], e_r.at[h], dev(x, yt, z, c),
            )
        sent_all(ev.at[h, 0:3], e_s.at[h])

    for cp in loads[2:]:
        cp.wait()
    eye = lax.broadcasted_iota(jnp.int32, (B, B), 0) == lax.broadcasted_iota(jnp.int32, (B, B), 1)
    for k in (2, 1, 0):
        for src, dst in ((tokens[k : k + 1, :].astype(F32), tc), (scales[k : k + 1, :], sc)):
            col = jnp.sum(jnp.where(eye, jnp.broadcast_to(src, (B, B)), 0.0), axis=1, keepdims=True)
            dst[k] = jnp.broadcast_to(col, (B, 128)).reshape(16, 16, 128)
        tok = tc[k].reshape(B, 128)
        for j in range(NY):
            base = ((j * NZ + z) * words).astype(F32)
            for t in range(words // 128):
                lane = lax.broadcasted_iota(jnp.int32, (B, 128), 1).astype(F32) + (base + 128.0 * t)
                at = j * words + t * 128
                hot[k, :, at : at + 128] = jnp.where(tok == lane, 1.0, 0.0).astype(BF)
    for k in range(STEPS):
        ft[:, k * B : (k + 1) * B] = fv[k].astype(F32).T.astype(BF)

    greet(rdy.at[3], x_near)
    for j in range(3):
        greet(rdy.at[j], z_near)
        pl.semaphore_wait(rdy.at[j], 2)
    pl.semaphore_wait(rdy.at[3], 2)

    def lookup(k, h):
        return jnp.dot(
            hot[k], ev[h].reshape(NY * words, hb), preferred_element_type=F32
        ).astype(BF).reshape(8, 32, hb)

    for h in range(2):
        loads[h].wait()
        arrive(ev.at[h, 0:3], e_r.at[h])
        x2[h] = lookup(2, h)
        for i in FAR:
            send(x2.at[h, zp(i)], rz2.at[h, i - 1], z2_s.at[h], z2_r.at[h], dev(x, y, zp(i), c))
        sent_all(rz2.at[h], z2_s.at[h])
        part = pl.multiple_of((sib if h == 0 else c) * (rows // 2), rows // 2)
        for lo in range(0, cols, 512):
            tt[h, lo : lo + 512, :] = tv[pl.ds(part, rows // 2), lo : lo + 512].astype(F32).T.astype(BF)

    for kk in (1, 0):
        for h in range(2):
            x10[kk, :, :, h * hb : (h + 1) * hb] = lookup(kk, h)

    def scaled(value, k, g):
        den = sc[k, g]
        return value / jnp.concatenate([den] * (value.shape[-1] // 128), axis=1)

    for h in range(2):
        tot = x2[h, z].astype(F32)
        arrive(rz2.at[h], z2_r.at[h])
        for i in NEAR:
            tot = tot + rz2[h, i - 1].astype(F32)
        tot = tot * bv[:, h * hb : (h + 1) * hb].astype(F32)
        ho = pl.ds(pl.multiple_of(y * blk + h * hb, hb), hb)
        for u in range(2):
            w[2, z // 2, 2 * (z % 2) + u, :, ho] = scaled(
                tot[u * 16 : (u + 1) * 16], 2, 2 * z + u
            ).astype(BF)
        mine = w.at[2, z // 2, pl.ds(2 * (z % 2), 2), :, ho]
        for i in FAR:
            send(mine, mine, zw_s.at[h], zw_r.at[h], dev(x, y, zp(i), c))
        sent_all(rz2.at[h], zw_s.at[h])

    def spread(kk):
        for i in FAR:
            send(
                x10.at[kk, zp(i)], rz10.at[kk, i - 1], z10_s.at[kk], z10_r.at[kk],
                dev(x, y, zp(i), c),
            )
        sent_all(rz10.at[kk], z10_s.at[kk])

    spread(1)
    three_a = w.at[2, 0:3, :, :, 0 : 4 * hb]
    for h in range(2):
        ho = pl.ds(pl.multiple_of(y * blk + h * hb, hb), hb)
        arrive(rz2.at[h], zw_r.at[h])
        if h == 0:
            part = w.at[2, :, :, :, ho]
            for i in (2, 1, 3):
                send(part, part, ya_s.at[0], ya_r.at[0], dev(x, yp(i), z, c))
            sent_all(three_a, ya_s.at[0])
    def y_part(k, t, yt):
        if k == 2:
            return w.at[2, :, t, :, pl.ds(pl.multiple_of(yt * blk + hb, hb), hb)]
        return w.at[k, yt, t]

    def y_three(k, t):
        return w.at[2, 0:3, t, :, 0 : 4 * hb] if k == 2 else w.at[k, 0:3, t]

    def y_send(k, t):
        part = y_part(k, t, y)
        for i in (2, 1, 3):
            send(part, part, y_s.at[k, t], y_r.at[k, t], dev(x, yp(i), z, c))
        sent_all(y_three(k, t), y_s.at[k, t])

    for t in range(NT):
        y_send(2, t)
    spread(0)

    def wait_rows(k, t):
        if k == 2 and t == 0:
            arrive(three_a, ya_r.at[0])
        arrive(y_three(k, t), y_r.at[k, t])

    def product(k, t, j):
        return jnp.dot(
            w[k, :, t].reshape(B // NT, cols), tt[j], preferred_element_type=F32
        ).reshape(4, 16, rows // 2)

    own_part = (x == y) & is_owner

    def rows_of(k, t, meanwhile=None):
        wait_rows(k + 1, t)
        pb[k, t] = product(k + 1, t, 0).astype(BF)
        send(pb.at[k, t], pr.at[k, t], pp_s.at[k, t], pp_r.at[k, t], dev(x, y, z, sib))
        sent_all(pb.at[k, t], pp_s.at[k, t])
        own[k, t] = product(k + 1, t, 1)
        if meanwhile is not None:
            meanwhile()
        arrive(pr.at[k, t], pp_r.at[k, t])
        qb[k, t] = (own[k, t] + pr[k, t].astype(F32)).astype(BF)
        for r in range(NY):
            self_r = (x == y) & (y == r) & is_owner
            send(
                qb.at[k, t, r], orx.at[k, t, x * 2 + c], o_s.at[k, t], o_r.at[k, t],
                dev(y, r, z, oc), jnp.logical_not(self_r),
            )

            @pl.when(self_r)
            def _():
                orx[k, t, x * 2 + c] = qb[k, t, r]

        sent_all(qb.at[k, t, 0:3], o_s.at[k, t], own_part)
        sent_all(qb.at[k, t], o_s.at[k, t], jnp.logical_not(own_part))

    pm_self = (y == z // 2) & (z == 4 * c + y)

    def tiles(kk):
        acc = x10[kk, z].astype(F32)
        arrive(rz10.at[kk], z10_r.at[kk])
        for i in NEAR:
            acc = acc + rz10[kk, i - 1].astype(F32)
        em_s[kk] = acc.astype(BF)
        send(
            em_s.at[kk], em.at[kk, z % 2], pm_s.at[kk], pm_r.at[kk, z % 2],
            dev(x, z // 2, 4 * c + y, c), jnp.logical_not(pm_self),
        )
        sent_all(em_s.at[kk], pm_s.at[kk], jnp.logical_not(pm_self))

        @pl.when(pm_self)
        def _():
            em[kk, z % 2] = em_s[kk]

    def tiles_done(kk):
        for h in range(2):
            from_self = (y == q) & (z == 2 * y + h)
            arrive(em.at[kk, h], pm_r.at[kk, h], is_owner & jnp.logical_not(from_self))

    def owner(k, t):
        arrive(orx.at[k, t, 0:7], o_r.at[k, t], own_part)
        arrive(orx.at[k, t], o_r.at[k, t], is_owner & jnp.logical_not(own_part))

        @pl.when(is_owner)
        def _():
            halves = []
            for cc in range(2):
                acc = orx[k, t, cc].astype(F32)
                for xx in range(1, NX):
                    acc = acc + orx[k, t, 2 * xx + cc].astype(F32)
                halves.append(acc)
            msg = jnp.concatenate(halves, axis=1).astype(BF).astype(F32)
            lo = 16 * (t % 2)
            w[k, y, t, :, pl.ds(qo, blk)] = scaled(
                em[k, t // 2, lo : lo + 16].astype(F32) * msg, k, 4 * y + t
            ).astype(BF)

        tile = w.at[k, y, t, :, pl.ds(qo, blk)]
        for i in FAR:
            send(tile, tile, zz_s.at[k, t], zz_r.at[k, t], dev(x, y, zp(i), c), is_owner)
        sent_all(rz2.at[0], zz_s.at[k, t], is_owner)

    def column(k, t):
        arrive(w.at[k, y, t, :, 0 : 3 * blk], zz_r.at[k, t], is_owner)
        arrive(w.at[k, y, t], zz_r.at[k, t], jnp.logical_not(is_owner))
        y_send(k, t)

    def last(t):
        wait_rows(0, t)
        for j, half in ((0, sib), (1, c)):
            fp[t, :, :, pl.ds(pl.multiple_of(half * (rows // 2), rows // 2), rows // 2)] = product(
                0, t, j
            )
        to = t // 2
        u = t % 2
        for i in (2, 1, 3, 0):
            send(
                fp.at[t, xp(i)], fx.at[u, 2 * i + c], fx_s.at[t], fx_r.at[u],
                dev(xp(i), y, z, to), c != to if i == 0 else None,
            )
        sent_all(fp.at[t], fx_s.at[t], c != to)
        sent_all(fp.at[t, 0:3], fx_s.at[t], c == to)

    rows_of(1, 0, lambda: tiles(1))
    rows_of(1, 1)
    rows_of(1, 2)
    tiles_done(1)
    owner(1, 0)
    rows_of(1, 3)
    owner(1, 1)
    owner(1, 2)
    column(1, 0)
    owner(1, 3)
    column(1, 1)
    tiles(0)
    column(1, 2)
    rows_of(0, 0)
    column(1, 3)
    rows_of(0, 1)
    rows_of(0, 2)
    tiles_done(0)
    owner(0, 0)
    rows_of(0, 3)
    owner(0, 1)
    owner(0, 2)
    column(0, 0)
    owner(0, 3)
    column(0, 1)
    column(0, 2)
    last(0)
    column(0, 3)
    last(1)
    last(2)
    last(3)

    def count_block(n):
        lo = n * 256
        acc = jnp.dot(
            ft[...], w[:, :, :, :, lo : lo + 256].reshape(STEPS * B, 256), preferred_element_type=F32
        )
        counts[:, lo : lo + 256] = tv[:, lo : lo + 256].astype(F32) * acc * (32.0 / (STEPS * B))

    for n in range(cols // 256):
        count_block(n)
    for u in range(2):
        tot = fp[2 * c + u, x]
        arrive(fx.at[u, 0:7], fx_r.at[u])
        for j in [sib] + list(range(2, 8)):
            tot = tot + fx[u, j]
        first[u * 16 : (u + 1) * 16] = tot
    for cond, size, sem in sent:
        wait = whole(size, sem).wait_send
        if cond is None:
            wait()
        else:
            pl.when(cond)(wait)


def per_device(*args):
    transition, emission = args[:2]
    rows, cols = transition.shape
    blk = cols // 4
    words = emission.shape[0]
    dma = pltpu.SemaphoreType.DMA
    vm = pltpu.VMEM
    hbm = pl.BlockSpec(memory_space=pltpu.HBM)
    vmem = pl.BlockSpec(memory_space=pltpu.VMEM)
    return pl.pallas_call(
        kernel,
        out_shape=(
            jax.ShapeDtypeStruct((rows, cols), F32),
            jax.ShapeDtypeStruct((B // 8, rows), F32),
        ),
        in_specs=[hbm] * 6,
        out_specs=(vmem, vmem),
        scratch_shapes=[
            vm((STEPS, B), F32),
            vm((STEPS, B), jnp.int32),
            vm((rows, cols), BF),
            vm((2, cols, rows // 2), BF),
            vm((2, NY, words, blk // 2), BF),
            vm((STEPS, B, rows), BF),
            vm((32, blk), BF),
            vm((rows, STEPS * B), BF),
            vm((STEPS, 16, 16, 128), F32),
            vm((STEPS, 16, 16, 128), F32),
            vm((STEPS, B, NY * words), BF),
            vm((2, 8, 32, blk // 2), BF),
            vm((2, 7, 32, blk // 2), BF),
            vm((2, 8, 32, blk), BF),
            vm((2, 7, 32, blk), BF),
            vm((2, 32, blk), BF),
            vm((2, 2, 32, blk), BF),
            vm((STEPS, 4, NT, 16, cols), BF),
            vm((2, NT, 4, 16, rows // 2), F32),
            vm((2, NT, 4, 16, rows // 2), BF),
            vm((2, NT, 4, 16, rows // 2), BF),
            vm((2, NT, 4, 16, rows // 2), BF),
            vm((2, NT, NX * NC, 16, rows // 2), BF),
            vm((NT, 4, 16, rows), F32),
            vm((2, NX * NC, 16, rows), F32),
            dma((7,)),
            pltpu.SemaphoreType.REGULAR((4,)),
            dma((2,)), dma((2,)),
            dma((2,)), dma((2,)),
            dma((2,)), dma((2,)),
            dma((2,)), dma((2,)),
            dma((2,)), dma((2, 2)),
            dma((1,)), dma((1,)),
            dma((3, NT)), dma((3, NT)),
            dma((2, NT)), dma((2, NT)),
            dma((2, NT)), dma((2, NT)),
            dma((2, NT)), dma((2, NT)),
            dma((NT,)), dma((2,)),
        ],
        compiler_params=pltpu.CompilerParams(
            collective_id=0, has_side_effects=True, vmem_limit_bytes=30 * 1024 * 1024
        ),
        name="window",
    )(*(pltpu.with_memory_space_constraint(a, pltpu.HBM) for a in args))


def solution(mesh):
    in_specs = (P("src", "dst"), P("src", "dst"), P(None, None, "src"), P(None, "dst"), P(), P())
    out_specs = (P("src", "dst"), P("dst", "src"))
    return jax.shard_map(
        per_device, mesh=mesh, in_specs=in_specs, out_specs=out_specs, check_vma=False
    )
```

```python
import jax
import jax.numpy as jnp
from jax import lax
from jax.experimental import pallas as pl
from jax.experimental.pallas import tpu as pltpu
from jax.sharding import PartitionSpec as P

MESH = pl.DeviceIdType.MESH
NX, NY, NZ, NC = 4, 4, 8, 2
B = 256
STEPS = 3
NT = 4
BF = jnp.bfloat16
F32 = jnp.float32
FAR = (4, 3, 5, 2, 6, 1, 7)
NEAR = (1, 7, 2, 6, 3, 5, 4)


def dev(x, y, z, c):
    return (y * NZ + z, x * NC + c)


def kernel(
    trans, emis, forw, beta, scales_in, tokens_in,
    counts, first,
    scales, tokens, tv, tt, ev, fv, bv, ft, sc, hot, eb, xb, rzb, sb, ryb,
    x2, rz2, x10, rz10, em_s, em,
    w, own, pb, pr, qb, orx, fp, fx,
    l_sem, rdy,
    e_s, e_r, zb_s, zb_r, yb_s, yb_r, z2_s, z2_r, zw_s, zw_r, z10_s, z10_r, pm_s, pm_r,
    ya_s, ya_r, y_s, y_r, pp_s, pp_r, o_s, o_r, zz_s, zz_r, fx_s, fx_r,
):
    s = lax.axis_index("src")
    d = lax.axis_index("dst")
    y, z = s // NZ, s % NZ
    x, c = d // NC, d % NC
    sib = 1 - c
    words = emis.shape[0]
    cols = emis.shape[1]
    blk = cols // 4
    hb = blk // 2
    qb_ = blk // 4
    rows = trans.shape[0]
    yo = pl.multiple_of(y * blk, blk)
    oc = z // 4
    q = z % 4
    qo = pl.multiple_of(q * blk, blk)
    is_owner = c == oc

    def zp(i):
        return lax.rem(z + i, NZ)

    def yp(i):
        return lax.rem(y + i, NY)

    def xp(i):
        return lax.rem(x + i, NX)

    barrier = pltpu.get_barrier_semaphore()
    z_near = [dev(x, y, zp(i), c) for i in (1, NZ - 1)]
    x_near = [dev(xp(i), y, z, c) for i in (1, NX - 1)]
    peers = [dev(x, y, z, sib)] + [dev(x, yp(i), z, c) for i in range(1, NY)] + z_near + x_near

    def greet(sem, to):
        for p in to:
            pl.semaphore_signal(sem, inc=1, device_id=p, device_id_type=MESH)

    greet(barrier, peers)
    loads = [
        pltpu.make_async_copy(emis.at[:, pl.ds(yo, hb)], ev.at[0, y], l_sem.at[0]),
        pltpu.make_async_copy(
            emis.at[:, pl.ds(pl.multiple_of(y * blk + hb, hb), hb)], ev.at[1, y], l_sem.at[1]
        ),
        pltpu.make_async_copy(
            beta.at[pl.ds(pl.multiple_of(z * 32, 32), 32), pl.ds(yo, blk)], bv, l_sem.at[2]
        ),
        pltpu.make_async_copy(trans, tv, l_sem.at[3]),
        pltpu.make_async_copy(forw, fv, l_sem.at[4]),
        pltpu.make_async_copy(scales_in, scales, l_sem.at[5]),
        pltpu.make_async_copy(tokens_in, tokens, l_sem.at[6]),
    ]
    corner = [
        pltpu.make_async_copy(
            emis.at[:, j * blk + hb + qb_ : (j + 1) * blk], eb.at[j], l_sem.at[7 + j]
        )
        for j in range(NY)
    ]
    for cp in loads[-1:] + corner + loads[:-1]:
        cp.start()
    pl.semaphore_wait(barrier, len(peers))

    sent = []

    def send(src, dst, ss, rs, to, cond=None):
        cp = pltpu.make_async_remote_copy(
            src_ref=src, dst_ref=dst, send_sem=ss, recv_sem=rs, device_id=to, device_id_type=MESH
        )
        if cond is None:
            cp.start()
        else:
            pl.when(cond)(cp.start)

    def sent_all(size, sem, cond=None):
        sent.append((cond, size, sem))

    here = dev(x, y, z, sib)

    def whole(size, sem):
        return pltpu.make_async_remote_copy(
            src_ref=size, dst_ref=size, send_sem=sem, recv_sem=sem,
            device_id=here, device_id_type=MESH,
        )

    def arrive(size, sem, cond=None):
        wait = whole(size, sem).wait_recv
        if cond is None:
            wait()
        else:
            pl.when(cond)(wait)

    for h, lo, at, size in ((0, 0, 0, hb), (1, hb, 0, qb_), (2, hb + qb_, qb_, qb_)):
        dst = ev.at[min(h, 1), y, :, at : at + size]
        for i in (2, 1, 3):
            yt = yp(i)
            send(
                emis.at[:, pl.ds(pl.multiple_of(yt * blk + lo, qb_), size)],
                dst, e_s.at[h], e_r.at[h], dev(x, yt, z, c),
            )
        sent_all(ev.at[0, 0:3, :, 0:size], e_s.at[h])

    eye = lax.broadcasted_iota(jnp.int32, (B, B), 0) == lax.broadcasted_iota(jnp.int32, (B, B), 1)

    def as_column(row):
        col = jnp.sum(jnp.where(eye, jnp.broadcast_to(row, (B, B)), 0.0), axis=1, keepdims=True)
        return jnp.broadcast_to(col, (B, 128))

    def hot_rows(k):
        tok = as_column(tokens[k : k + 1, :].astype(F32))
        for j in range(NY):
            base = ((j * NZ + z) * words).astype(F32)
            for t in range(words // 128):
                lane = lax.broadcasted_iota(jnp.int32, (B, 128), 1).astype(F32) + (base + 128.0 * t)
                at = j * words + t * 128
                hot[k, :, at : at + 128] = jnp.where(tok == lane, 1.0, 0.0).astype(BF)

    loads[6].wait()
    hot_rows(2)
    for cp in corner:
        cp.wait()
    mine_hot = hot[2, :, pl.ds(pl.multiple_of(y * words, words), words)]
    for j in range(NY):
        xb[:, j] = (
            jnp.dot(mine_hot, eb[j], preferred_element_type=F32).astype(BF).reshape(8, 32, qb_)
        )
    for j in range(3):
        greet(rdy.at[j], z_near)
        pl.semaphore_wait(rdy.at[j], 2)
    for i in FAR:
        send(xb.at[zp(i)], rzb.at[i - 1], zb_s.at[0], zb_r.at[0], dev(x, y, zp(i), c))
    sent_all(rzb, zb_s.at[0])

    for cp in loads[2:6]:
        cp.wait()
    for k in (2, 1, 0):
        sc[k] = as_column(scales[k : k + 1, :]).reshape(16, 16, 128)
        if k < 2:
            hot_rows(k)
    for k in range(STEPS):
        ft[:, k * B : (k + 1) * B] = fv[k].astype(F32).T.astype(BF)
    greet(rdy.at[3], x_near)
    pl.semaphore_wait(rdy.at[3], 2)

    def lookup(k, h, size):
        return jnp.dot(
            hot[k], ev[h, :, :, 0:size].reshape(NY * words, size), preferred_element_type=F32
        ).astype(BF).reshape(8, 32, size)

    for h, size in ((0, hb), (1, qb_)):
        loads[h].wait()
        arrive(ev.at[0, 0:3, :, 0:size], e_r.at[h])
        x2[h, :, :, 0:size] = lookup(2, h, size)
        for i in FAR:
            send(
                x2.at[h, zp(i), :, 0:size], rz2.at[h, i - 1, :, 0:size], z2_s.at[h], z2_r.at[h],
                dev(x, y, zp(i), c),
            )
        sent_all(rz2.at[h, :, :, 0:size], z2_s.at[h])
        part = pl.multiple_of((sib if h == 0 else c) * (rows // 2), rows // 2)
        for lo in range(0, cols, 512):
            tt[h, lo : lo + 512, :] = tv[pl.ds(part, rows // 2), lo : lo + 512].astype(F32).T.astype(BF)
    arrive(rzb, zb_r.at[0])
    tot = xb[z].astype(F32)
    for i in range(7):
        tot = tot + rzb[i].astype(F32)
    sb[...] = tot.astype(BF)
    for i in (2, 1, 3):
        send(sb.at[yp(i)], ryb.at[i - 1], yb_s.at[0], yb_r.at[0], dev(x, yp(i), z, c))
    sent_all(ryb, yb_s.at[0])
    arrive(ev.at[0, 0:3, :, 0:qb_], e_r.at[2])
    for kk in (1, 0):
        for h in range(2):
            x10[kk, :, :, h * hb : (h + 1) * hb] = lookup(kk, h, hb)

    def scaled(value, k, g):
        den = sc[k, g]
        return value / jnp.concatenate([den] * (value.shape[-1] // 128), axis=1)

    for h in range(2):
        size = (hb, qb_)[h]
        tot = x2[h, z, :, 0:size].astype(F32)
        arrive(rz2.at[h, :, :, 0:size], z2_r.at[h])
        for i in NEAR:
            tot = tot + rz2[h, i - 1, :, 0:size].astype(F32)
        if h == 1:
            arrive(ryb, yb_r.at[0])
            rest = sb[y].astype(F32)
            for i in range(3):
                rest = rest + ryb[i].astype(F32)
            tot = jnp.concatenate([tot, rest], axis=1)
        tot = tot * bv[:, h * hb : (h + 1) * hb].astype(F32)
        ho = pl.ds(pl.multiple_of(y * blk + h * hb, hb), hb)
        for u in range(2):
            w[2, z // 2, 2 * (z % 2) + u, :, ho] = scaled(
                tot[u * 16 : (u + 1) * 16], 2, 2 * z + u
            ).astype(BF)
        mine = w.at[2, z // 2, pl.ds(2 * (z % 2), 2), :, ho]
        for i in FAR:
            send(mine, mine, zw_s.at[h], zw_r.at[h], dev(x, y, zp(i), c))
        sent_all(rz2.at[h], zw_s.at[h])

    def spread(kk):
        for i in FAR:
            send(
                x10.at[kk, zp(i)], rz10.at[kk, i - 1], z10_s.at[kk], z10_r.at[kk],
                dev(x, y, zp(i), c),
            )
        sent_all(rz10.at[kk], z10_s.at[kk])

    spread(1)
    three_a = w.at[2, 0:3, :, :, 0 : 4 * hb]
    for h in range(2):
        ho = pl.ds(pl.multiple_of(y * blk + h * hb, hb), hb)
        arrive(rz2.at[h], zw_r.at[h])
        if h == 0:
            part = w.at[2, :, :, :, ho]
            for i in (2, 1, 3):
                send(part, part, ya_s.at[0], ya_r.at[0], dev(x, yp(i), z, c))
            sent_all(three_a, ya_s.at[0])
    def y_part(k, t, yt):
        if k == 2:
            return w.at[2, :, t, :, pl.ds(pl.multiple_of(yt * blk + hb, hb), hb)]
        return w.at[k, yt, t]

    def y_three(k, t):
        return w.at[2, 0:3, t, :, 0 : 4 * hb] if k == 2 else w.at[k, 0:3, t]

    def y_send(k, t):
        part = y_part(k, t, y)
        for i in (2, 1, 3):
            send(part, part, y_s.at[k, t], y_r.at[k, t], dev(x, yp(i), z, c))
        sent_all(y_three(k, t), y_s.at[k, t])

    for t in range(NT):
        y_send(2, t)
    spread(0)

    def wait_rows(k, t):
        if k == 2 and t == 0:
            arrive(three_a, ya_r.at[0])
        arrive(y_three(k, t), y_r.at[k, t])

    def product(k, t, j):
        return jnp.dot(
            w[k, :, t].reshape(B // NT, cols), tt[j], preferred_element_type=F32
        ).reshape(4, 16, rows // 2)

    own_part = (x == y) & is_owner

    def partial_sums(k, t):
        wait_rows(k + 1, t)
        theirs, ours = product(k + 1, t, 0), product(k + 1, t, 1)
        pb[k, t] = theirs.astype(BF)
        own[k, t] = ours
        send(pb.at[k, t], pr.at[k, t], pp_s.at[k, t], pp_r.at[k, t], dev(x, y, z, sib))
        sent_all(pb.at[k, t], pp_s.at[k, t])

    def pair_sums(k, t):
        arrive(pr.at[k, t], pp_r.at[k, t])
        qb[k, t] = (own[k, t] + pr[k, t].astype(F32)).astype(BF)
        for r in range(NY):
            self_r = (x == y) & (y == r) & is_owner
            send(
                qb.at[k, t, r], orx.at[k, t, x * 2 + c], o_s.at[k, t], o_r.at[k, t],
                dev(y, r, z, oc), jnp.logical_not(self_r),
            )

            @pl.when(self_r)
            def _():
                orx[k, t, x * 2 + c] = qb[k, t, r]

        sent_all(qb.at[k, t, 0:3], o_s.at[k, t], own_part)
        sent_all(qb.at[k, t], o_s.at[k, t], jnp.logical_not(own_part))

    pm_self = (y == z // 2) & (z == 4 * c + y)

    def tiles(kk):
        acc = x10[kk, z].astype(F32)
        arrive(rz10.at[kk], z10_r.at[kk])
        for i in NEAR:
            acc = acc + rz10[kk, i - 1].astype(F32)
        em_s[kk] = acc.astype(BF)
        send(
            em_s.at[kk], em.at[kk, z % 2], pm_s.at[kk], pm_r.at[kk, z % 2],
            dev(x, z // 2, 4 * c + y, c), jnp.logical_not(pm_self),
        )
        sent_all(em_s.at[kk], pm_s.at[kk], jnp.logical_not(pm_self))

        @pl.when(pm_self)
        def _():
            em[kk, z % 2] = em_s[kk]

    def tiles_done(kk):
        for h in range(2):
            from_self = (y == q) & (z == 2 * y + h)
            arrive(em.at[kk, h], pm_r.at[kk, h], is_owner & jnp.logical_not(from_self))

    def owner(k, t):
        arrive(orx.at[k, t, 0:7], o_r.at[k, t], own_part)
        arrive(orx.at[k, t], o_r.at[k, t], is_owner & jnp.logical_not(own_part))

        @pl.when(is_owner)
        def _():
            halves = []
            for cc in range(2):
                acc = orx[k, t, cc].astype(F32)
                for xx in range(1, NX):
                    acc = acc + orx[k, t, 2 * xx + cc].astype(F32)
                halves.append(acc)
            msg = jnp.concatenate(halves, axis=1).astype(BF).astype(F32)
            lo = 16 * (t % 2)
            w[k, y, t, :, pl.ds(qo, blk)] = scaled(
                em[k, t // 2, lo : lo + 16].astype(F32) * msg, k, 4 * y + t
            ).astype(BF)

        tile = w.at[k, y, t, :, pl.ds(qo, blk)]
        for i in FAR:
            send(tile, tile, zz_s.at[k, t], zz_r.at[k, t], dev(x, y, zp(i), c), is_owner)
        sent_all(rz2.at[0], zz_s.at[k, t], is_owner)

    def column(k, t):
        arrive(w.at[k, y, t, :, 0 : 3 * blk], zz_r.at[k, t], is_owner)
        arrive(w.at[k, y, t], zz_r.at[k, t], jnp.logical_not(is_owner))
        y_send(k, t)

    def last(t):
        wait_rows(0, t)
        for j, half in ((0, sib), (1, c)):
            fp[t, :, :, pl.ds(pl.multiple_of(half * (rows // 2), rows // 2), rows // 2)] = product(
                0, t, j
            )
        to = t // 2
        u = t % 2
        for i in (2, 1, 3, 0):
            send(
                fp.at[t, xp(i)], fx.at[u, 2 * i + c], fx_s.at[t], fx_r.at[u],
                dev(xp(i), y, z, to), c != to if i == 0 else None,
            )
        sent_all(fp.at[t], fx_s.at[t], c != to)
        sent_all(fp.at[t, 0:3], fx_s.at[t], c == to)

    partial_sums(1, 0)
    tiles(1)
    pair_sums(1, 0)
    partial_sums(1, 1)
    partial_sums(1, 2)
    pair_sums(1, 1)
    partial_sums(1, 3)
    pair_sums(1, 2)
    pair_sums(1, 3)
    tiles_done(1)
    owner(1, 0)
    owner(1, 1)
    owner(1, 2)
    column(1, 0)
    owner(1, 3)
    column(1, 1)
    tiles(0)
    column(1, 2)
    partial_sums(0, 0)
    pair_sums(0, 0)
    column(1, 3)
    partial_sums(0, 1)
    pair_sums(0, 1)
    partial_sums(0, 2)
    pair_sums(0, 2)
    tiles_done(0)
    owner(0, 0)
    partial_sums(0, 3)
    pair_sums(0, 3)
    owner(0, 1)
    owner(0, 2)
    column(0, 0)
    owner(0, 3)
    column(0, 1)
    column(0, 2)
    last(0)
    column(0, 3)
    last(1)
    last(2)
    last(3)

    def count_block(n):
        lo = n * 256
        acc = jnp.dot(
            ft[...], w[:, :, :, :, lo : lo + 256].reshape(STEPS * B, 256), preferred_element_type=F32
        )
        counts[:, lo : lo + 256] = tv[:, lo : lo + 256].astype(F32) * acc * (32.0 / (STEPS * B))

    for n in range(cols // 256):
        count_block(n)
    for u in range(2):
        tot = fp[2 * c + u, x]
        arrive(fx.at[u, 0:7], fx_r.at[u])
        for j in [sib] + list(range(2, 8)):
            tot = tot + fx[u, j]
        first[u * 16 : (u + 1) * 16] = tot
    for cond, size, sem in sent:
        wait = whole(size, sem).wait_send
        if cond is None:
            wait()
        else:
            pl.when(cond)(wait)


def per_device(*args):
    transition, emission = args[:2]
    rows, cols = transition.shape
    blk = cols // 4
    words = emission.shape[0]
    dma = pltpu.SemaphoreType.DMA
    vm = pltpu.VMEM
    hbm = pl.BlockSpec(memory_space=pltpu.HBM)
    vmem = pl.BlockSpec(memory_space=pltpu.VMEM)
    return pl.pallas_call(
        kernel,
        out_shape=(
            jax.ShapeDtypeStruct((rows, cols), F32),
            jax.ShapeDtypeStruct((B // 8, rows), F32),
        ),
        in_specs=[hbm] * 6,
        out_specs=(vmem, vmem),
        scratch_shapes=[
            vm((STEPS, B), F32),
            vm((STEPS, B), jnp.int32),
            vm((rows, cols), BF),
            vm((2, cols, rows // 2), BF),
            vm((2, NY, words, blk // 2), BF),
            vm((STEPS, B, rows), BF),
            vm((32, blk), BF),
            vm((rows, STEPS * B), BF),
            vm((STEPS, 16, 16, 128), F32),
            vm((STEPS, B, NY * words), BF),
            vm((NY, words, blk // 4), BF),
            vm((8, NY, 32, blk // 4), BF),
            vm((7, NY, 32, blk // 4), BF),
            vm((NY, 32, blk // 4), BF),
            vm((3, 32, blk // 4), BF),
            vm((2, 8, 32, blk // 2), BF),
            vm((2, 7, 32, blk // 2), BF),
            vm((2, 8, 32, blk), BF),
            vm((2, 7, 32, blk), BF),
            vm((2, 32, blk), BF),
            vm((2, 2, 32, blk), BF),
            vm((STEPS, 4, NT, 16, cols), BF),
            vm((2, NT, 4, 16, rows // 2), F32),
            vm((2, NT, 4, 16, rows // 2), BF),
            vm((2, NT, 4, 16, rows // 2), BF),
            vm((2, NT, 4, 16, rows // 2), BF),
            vm((2, NT, NX * NC, 16, rows // 2), BF),
            vm((NT, 4, 16, rows), F32),
            vm((2, NX * NC, 16, rows), F32),
            dma((11,)),
            pltpu.SemaphoreType.REGULAR((4,)),
            dma((3,)), dma((3,)),
            dma((1,)), dma((1,)),
            dma((1,)), dma((1,)),
            dma((2,)), dma((2,)),
            dma((2,)), dma((2,)),
            dma((2,)), dma((2,)),
            dma((2,)), dma((2, 2)),
            dma((1,)), dma((1,)),
            dma((3, NT)), dma((3, NT)),
            dma((2, NT)), dma((2, NT)),
            dma((2, NT)), dma((2, NT)),
            dma((2, NT)), dma((2, NT)),
            dma((NT,)), dma((2,)),
        ],
        compiler_params=pltpu.CompilerParams(
            collective_id=0, has_side_effects=True, vmem_limit_bytes=30 * 1024 * 1024
        ),
        name="window",
    )(*(pltpu.with_memory_space_constraint(a, pltpu.HBM) for a in args))


def solution(mesh):
    in_specs = (P("src", "dst"), P("src", "dst"), P(None, None, "src"), P(None, "dst"), P(), P())
    out_specs = (P("src", "dst"), P("dst", "src"))
    return jax.shard_map(
        per_device, mesh=mesh, in_specs=in_specs, out_specs=out_specs, check_vma=False
    )
```

```python
import jax
import jax.numpy as jnp
from jax import lax
from jax.experimental import pallas as pl
from jax.experimental.pallas import tpu as pltpu
from jax.sharding import PartitionSpec as P

MESH = pl.DeviceIdType.MESH
NX, NY, NZ, NC = 4, 4, 8, 2
B = 256
STEPS = 3
NT = 4
BF = jnp.bfloat16
F32 = jnp.float32
FAR = (4, 3, 5, 2, 6, 1, 7)
NEAR = (1, 7, 2, 6, 3, 5, 4)


def dev(x, y, z, c):
    return (y * NZ + z, x * NC + c)


def kernel(
    trans, emis, forw, beta, scales_in, tokens_in,
    counts, first,
    scales, tokens, tv, tt, ev, fv, bv, ft, sc, hot, eb, xb, rzb, sb, ryb,
    x2, rz2, x10, rz10, em_s, em,
    w, own, pb, pr, qb, orx, fp, fx,
    l_sem, rdy,
    e_s, e_r, zb_s, zb_r, yb_s, yb_r, z2_s, z2_r, zw_s, zw_r, z10_s, z10_r, pm_s, pm_r,
    ya_s, ya_r, y_s, y_r, pp_s, pp_r, o_s, o_r, zz_s, zz_r, fx_s, fx_r,
):
    s = lax.axis_index("src")
    d = lax.axis_index("dst")
    y, z = s // NZ, s % NZ
    x, c = d // NC, d % NC
    sib = 1 - c
    words = emis.shape[0]
    cols = emis.shape[1]
    blk = cols // 4
    hb = blk // 2
    qb_ = blk // 4
    rows = trans.shape[0]
    yo = pl.multiple_of(y * blk, blk)
    oc = z // 4
    q = z % 4
    qo = pl.multiple_of(q * blk, blk)
    is_owner = c == oc

    def zp(i):
        return lax.rem(z + i, NZ)

    def yp(i):
        return lax.rem(y + i, NY)

    def xp(i):
        return lax.rem(x + i, NX)

    barrier = pltpu.get_barrier_semaphore()
    z_near = [dev(x, y, zp(i), c) for i in (1, NZ - 1)]
    x_near = [dev(xp(i), y, z, c) for i in (1, NX - 1)]
    peers = [dev(x, y, z, sib)] + [dev(x, yp(i), z, c) for i in range(1, NY)] + z_near + x_near

    def greet(sem, to):
        for p in to:
            pl.semaphore_signal(sem, inc=1, device_id=p, device_id_type=MESH)

    greet(barrier, peers)
    loads = [
        pltpu.make_async_copy(emis.at[:, pl.ds(yo, hb)], ev.at[0, y], l_sem.at[0]),
        pltpu.make_async_copy(
            emis.at[:, pl.ds(pl.multiple_of(y * blk + hb, hb), hb)], ev.at[1, y], l_sem.at[1]
        ),
        pltpu.make_async_copy(
            beta.at[pl.ds(pl.multiple_of(z * 32, 32), 32), pl.ds(yo, blk)], bv, l_sem.at[2]
        ),
        pltpu.make_async_copy(trans, tv, l_sem.at[3]),
        pltpu.make_async_copy(forw, fv, l_sem.at[4]),
        pltpu.make_async_copy(scales_in, scales, l_sem.at[5]),
        pltpu.make_async_copy(tokens_in, tokens, l_sem.at[6]),
    ]
    corner = [
        pltpu.make_async_copy(
            emis.at[:, j * blk + hb + qb_ : (j + 1) * blk], eb.at[j], l_sem.at[7 + j]
        )
        for j in range(NY)
    ]
    for cp in loads[-1:] + corner + loads[:-1]:
        cp.start()
    pl.semaphore_wait(barrier, len(peers))

    sent = []

    def send(src, dst, ss, rs, to, cond=None):
        cp = pltpu.make_async_remote_copy(
            src_ref=src, dst_ref=dst, send_sem=ss, recv_sem=rs, device_id=to, device_id_type=MESH
        )
        if cond is None:
            cp.start()
        else:
            pl.when(cond)(cp.start)

    def sent_all(size, sem, cond=None):
        sent.append((cond, size, sem))

    here = dev(x, y, z, sib)

    def whole(size, sem):
        return pltpu.make_async_remote_copy(
            src_ref=size, dst_ref=size, send_sem=sem, recv_sem=sem,
            device_id=here, device_id_type=MESH,
        )

    def arrive(size, sem, cond=None):
        wait = whole(size, sem).wait_recv
        if cond is None:
            wait()
        else:
            pl.when(cond)(wait)

    for h, lo, at, size in ((0, 0, 0, hb), (1, hb, 0, qb_), (2, hb + qb_, qb_, qb_)):
        dst = ev.at[min(h, 1), y, :, at : at + size]
        for i in (2, 1, 3):
            yt = yp(i)
            send(
                emis.at[:, pl.ds(pl.multiple_of(yt * blk + lo, qb_), size)],
                dst, e_s.at[h], e_r.at[h], dev(x, yt, z, c),
            )
        sent_all(ev.at[0, 0:3, :, 0:size], e_s.at[h])

    eye = lax.broadcasted_iota(jnp.int32, (B, B), 0) == lax.broadcasted_iota(jnp.int32, (B, B), 1)

    def as_column(row):
        col = jnp.sum(jnp.where(eye, jnp.broadcast_to(row, (B, B)), 0.0), axis=1, keepdims=True)
        return jnp.broadcast_to(col, (B, 128))

    def hot_rows(k):
        tok = as_column(tokens[k : k + 1, :].astype(F32))
        for j in range(NY):
            base = ((j * NZ + z) * words).astype(F32)
            for t in range(words // 128):
                lane = lax.broadcasted_iota(jnp.int32, (B, 128), 1).astype(F32) + (base + 128.0 * t)
                at = j * words + t * 128
                hot[k, :, at : at + 128] = jnp.where(tok == lane, 1.0, 0.0).astype(BF)

    def greet_ring(j):
        greet(rdy.at[j], z_near)

    def greeted_ring(j):
        pl.semaphore_wait(rdy.at[j], 2)

    greet_ring(0)
    greet(rdy.at[3], x_near)
    loads[6].wait()
    hot_rows(2)
    for cp in corner:
        cp.wait()
    mine_hot = hot[2, :, pl.ds(pl.multiple_of(y * words, words), words)]
    for j in range(NY):
        if j in (0, 2):
            greeted_ring(j // 2)
            greet_ring(j // 2 + 1)
        xb[:, j] = (
            jnp.dot(mine_hot, eb[j], preferred_element_type=F32).astype(BF).reshape(8, 32, qb_)
        )
    greeted_ring(2)
    for i in FAR:
        send(xb.at[zp(i)], rzb.at[i - 1], zb_s.at[0], zb_r.at[0], dev(x, y, zp(i), c))
    sent_all(rzb, zb_s.at[0])

    for k in (1, 0):
        hot_rows(k)
    for cp in loads[2:6]:
        cp.wait()
    sc[2] = as_column(scales[2:3, :]).reshape(16, 16, 128)
    pl.semaphore_wait(rdy.at[3], 2)

    def lookup(k, h, size):
        return jnp.dot(
            hot[k], ev[h, :, :, 0:size].reshape(NY * words, size), preferred_element_type=F32
        ).astype(BF).reshape(8, 32, size)

    for h, size in ((0, hb), (1, qb_)):
        loads[h].wait()
        arrive(ev.at[0, 0:3, :, 0:size], e_r.at[h])
        x2[h, :, :, 0:size] = lookup(2, h, size)
        for i in FAR:
            send(
                x2.at[h, zp(i), :, 0:size], rz2.at[h, i - 1, :, 0:size], z2_s.at[h], z2_r.at[h],
                dev(x, y, zp(i), c),
            )
        sent_all(rz2.at[h, :, :, 0:size], z2_s.at[h])
        part = pl.multiple_of((sib if h == 0 else c) * (rows // 2), rows // 2)
        for lo in range(0, cols, 512):
            tt[h, lo : lo + 512, :] = tv[pl.ds(part, rows // 2), lo : lo + 512].astype(F32).T.astype(BF)
    arrive(rzb, zb_r.at[0])
    tot = xb[z].astype(F32)
    for i in range(7):
        tot = tot + rzb[i].astype(F32)
    sb[...] = tot.astype(BF)
    for i in (2, 1, 3):
        send(sb.at[yp(i)], ryb.at[i - 1], yb_s.at[0], yb_r.at[0], dev(x, yp(i), z, c))
    sent_all(ryb, yb_s.at[0])
    arrive(ev.at[0, 0:3, :, 0:qb_], e_r.at[2])
    for kk in (1, 0):
        for h in range(2):
            x10[kk, :, :, h * hb : (h + 1) * hb] = lookup(kk, h, hb)

    def scaled(value, k, g):
        den = sc[k, g]
        return value / jnp.concatenate([den] * (value.shape[-1] // 128), axis=1)

    for h in range(2):
        size = (hb, qb_)[h]
        tot = x2[h, z, :, 0:size].astype(F32)
        arrive(rz2.at[h, :, :, 0:size], z2_r.at[h])
        for i in NEAR:
            tot = tot + rz2[h, i - 1, :, 0:size].astype(F32)
        if h == 1:
            arrive(ryb, yb_r.at[0])
            rest = sb[y].astype(F32)
            for i in range(3):
                rest = rest + ryb[i].astype(F32)
            tot = jnp.concatenate([tot, rest], axis=1)
        tot = tot * bv[:, h * hb : (h + 1) * hb].astype(F32)
        ho = pl.ds(pl.multiple_of(y * blk + h * hb, hb), hb)
        for u in range(2):
            w[2, z // 2, 2 * (z % 2) + u, :, ho] = scaled(
                tot[u * 16 : (u + 1) * 16], 2, 2 * z + u
            ).astype(BF)
        mine = w.at[2, z // 2, pl.ds(2 * (z % 2), 2), :, ho]
        for i in FAR:
            send(mine, mine, zw_s.at[h], zw_r.at[h], dev(x, y, zp(i), c))
        sent_all(rz2.at[h], zw_s.at[h])

    def spread(kk):
        for i in FAR:
            send(
                x10.at[kk, zp(i)], rz10.at[kk, i - 1], z10_s.at[kk], z10_r.at[kk],
                dev(x, y, zp(i), c),
            )
        sent_all(rz10.at[kk], z10_s.at[kk])

    spread(1)
    three_a = w.at[2, 0:3, :, :, 0 : 4 * hb]
    for h in range(2):
        ho = pl.ds(pl.multiple_of(y * blk + h * hb, hb), hb)
        arrive(rz2.at[h], zw_r.at[h])
        if h == 0:
            part = w.at[2, :, :, :, ho]
            for i in (2, 1, 3):
                send(part, part, ya_s.at[0], ya_r.at[0], dev(x, yp(i), z, c))
            sent_all(three_a, ya_s.at[0])
    def y_part(k, t, yt):
        if k == 2:
            return w.at[2, :, t, :, pl.ds(pl.multiple_of(yt * blk + hb, hb), hb)]
        return w.at[k, yt, t]

    def y_three(k, t):
        return w.at[2, 0:3, t, :, 0 : 4 * hb] if k == 2 else w.at[k, 0:3, t]

    def y_send(k, t):
        part = y_part(k, t, y)
        for i in (2, 1, 3):
            send(part, part, y_s.at[k, t], y_r.at[k, t], dev(x, yp(i), z, c))
        sent_all(y_three(k, t), y_s.at[k, t])

    for t in range(NT):
        y_send(2, t)
    spread(0)
    for k in (1, 0):
        sc[k] = as_column(scales[k : k + 1, :]).reshape(16, 16, 128)
    for k in range(STEPS):
        ft[:, k * B : (k + 1) * B] = fv[k].astype(F32).T.astype(BF)

    def wait_rows(k, t):
        if k == 2 and t == 0:
            arrive(three_a, ya_r.at[0])
        arrive(y_three(k, t), y_r.at[k, t])

    def product(k, t, j):
        return jnp.dot(
            w[k, :, t].reshape(B // NT, cols), tt[j], preferred_element_type=F32
        ).reshape(4, 16, rows // 2)

    own_part = (x == y) & is_owner

    def partial_sums(k, t):
        wait_rows(k + 1, t)
        theirs, ours = product(k + 1, t, 0), product(k + 1, t, 1)
        pb[k, t] = theirs.astype(BF)
        own[k, t] = ours
        send(pb.at[k, t], pr.at[k, t], pp_s.at[k, t], pp_r.at[k, t], dev(x, y, z, sib))
        sent_all(pb.at[k, t], pp_s.at[k, t])

    def pair_sums(k, t):
        arrive(pr.at[k, t], pp_r.at[k, t])
        qb[k, t] = (own[k, t] + pr[k, t].astype(F32)).astype(BF)
        for r in range(NY):
            self_r = (x == y) & (y == r) & is_owner
            send(
                qb.at[k, t, r], orx.at[k, t, x * 2 + c], o_s.at[k, t], o_r.at[k, t],
                dev(y, r, z, oc), jnp.logical_not(self_r),
            )

            @pl.when(self_r)
            def _():
                orx[k, t, x * 2 + c] = qb[k, t, r]

        sent_all(qb.at[k, t, 0:3], o_s.at[k, t], own_part)
        sent_all(qb.at[k, t], o_s.at[k, t], jnp.logical_not(own_part))

    pm_self = (y == z // 2) & (z == 4 * c + y)

    def tiles(kk):
        acc = x10[kk, z].astype(F32)
        arrive(rz10.at[kk], z10_r.at[kk])
        for i in NEAR:
            acc = acc + rz10[kk, i - 1].astype(F32)
        em_s[kk] = acc.astype(BF)
        send(
            em_s.at[kk], em.at[kk, z % 2], pm_s.at[kk], pm_r.at[kk, z % 2],
            dev(x, z // 2, 4 * c + y, c), jnp.logical_not(pm_self),
        )
        sent_all(em_s.at[kk], pm_s.at[kk], jnp.logical_not(pm_self))

        @pl.when(pm_self)
        def _():
            em[kk, z % 2] = em_s[kk]

    def tiles_done(kk):
        for h in range(2):
            from_self = (y == q) & (z == 2 * y + h)
            arrive(em.at[kk, h], pm_r.at[kk, h], is_owner & jnp.logical_not(from_self))

    def owner(k, t):
        arrive(orx.at[k, t, 0:7], o_r.at[k, t], own_part)
        arrive(orx.at[k, t], o_r.at[k, t], is_owner & jnp.logical_not(own_part))

        @pl.when(is_owner)
        def _():
            halves = []
            for cc in range(2):
                acc = orx[k, t, cc].astype(F32)
                for xx in range(1, NX):
                    acc = acc + orx[k, t, 2 * xx + cc].astype(F32)
                halves.append(acc)
            msg = jnp.concatenate(halves, axis=1).astype(BF).astype(F32)
            lo = 16 * (t % 2)
            w[k, y, t, :, pl.ds(qo, blk)] = scaled(
                em[k, t // 2, lo : lo + 16].astype(F32) * msg, k, 4 * y + t
            ).astype(BF)

        tile = w.at[k, y, t, :, pl.ds(qo, blk)]
        for i in FAR:
            send(tile, tile, zz_s.at[k, t], zz_r.at[k, t], dev(x, y, zp(i), c), is_owner)
        sent_all(rz2.at[0], zz_s.at[k, t], is_owner)

    def column(k, t):
        arrive(w.at[k, y, t, :, 0 : 3 * blk], zz_r.at[k, t], is_owner)
        arrive(w.at[k, y, t], zz_r.at[k, t], jnp.logical_not(is_owner))
        y_send(k, t)

    def last(t):
        wait_rows(0, t)
        for j, half in ((0, sib), (1, c)):
            fp[t, :, :, pl.ds(pl.multiple_of(half * (rows // 2), rows // 2), rows // 2)] = product(
                0, t, j
            )
        to = t // 2
        u = t % 2
        for i in (2, 1, 3, 0):
            send(
                fp.at[t, xp(i)], fx.at[u, 2 * i + c], fx_s.at[t], fx_r.at[u],
                dev(xp(i), y, z, to), c != to if i == 0 else None,
            )
        sent_all(fp.at[t], fx_s.at[t], c != to)
        sent_all(fp.at[t, 0:3], fx_s.at[t], c == to)

    partial_sums(1, 0)
    tiles(1)
    pair_sums(1, 0)
    partial_sums(1, 1)
    partial_sums(1, 2)
    pair_sums(1, 1)
    partial_sums(1, 3)
    pair_sums(1, 2)
    pair_sums(1, 3)
    tiles_done(1)
    owner(1, 0)
    owner(1, 1)
    owner(1, 2)
    column(1, 0)
    owner(1, 3)
    column(1, 1)
    tiles(0)
    column(1, 2)
    partial_sums(0, 0)
    pair_sums(0, 0)
    column(1, 3)
    partial_sums(0, 1)
    pair_sums(0, 1)
    partial_sums(0, 2)
    pair_sums(0, 2)
    tiles_done(0)
    owner(0, 0)
    partial_sums(0, 3)
    pair_sums(0, 3)
    owner(0, 1)
    owner(0, 2)
    column(0, 0)
    owner(0, 3)
    column(0, 1)
    column(0, 2)
    last(0)
    column(0, 3)
    last(1)
    last(2)
    last(3)

    def count_block(n):
        lo = n * 256
        acc = jnp.dot(
            ft[...], w[:, :, :, :, lo : lo + 256].reshape(STEPS * B, 256), preferred_element_type=F32
        )
        counts[:, lo : lo + 256] = tv[:, lo : lo + 256].astype(F32) * acc * (32.0 / (STEPS * B))

    for n in range(cols // 256):
        count_block(n)
    for u in range(2):
        tot = fp[2 * c + u, x]
        arrive(fx.at[u, 0:7], fx_r.at[u])
        for j in [sib] + list(range(2, 8)):
            tot = tot + fx[u, j]
        first[u * 16 : (u + 1) * 16] = tot
    for cond, size, sem in sent:
        wait = whole(size, sem).wait_send
        if cond is None:
            wait()
        else:
            pl.when(cond)(wait)


def per_device(*args):
    transition, emission = args[:2]
    rows, cols = transition.shape
    blk = cols // 4
    words = emission.shape[0]
    dma = pltpu.SemaphoreType.DMA
    vm = pltpu.VMEM
    hbm = pl.BlockSpec(memory_space=pltpu.HBM)
    vmem = pl.BlockSpec(memory_space=pltpu.VMEM)
    return pl.pallas_call(
        kernel,
        out_shape=(
            jax.ShapeDtypeStruct((rows, cols), F32),
            jax.ShapeDtypeStruct((B // 8, rows), F32),
        ),
        in_specs=[hbm] * 6,
        out_specs=(vmem, vmem),
        scratch_shapes=[
            vm((STEPS, B), F32),
            vm((STEPS, B), jnp.int32),
            vm((rows, cols), BF),
            vm((2, cols, rows // 2), BF),
            vm((2, NY, words, blk // 2), BF),
            vm((STEPS, B, rows), BF),
            vm((32, blk), BF),
            vm((rows, STEPS * B), BF),
            vm((STEPS, 16, 16, 128), F32),
            vm((STEPS, B, NY * words), BF),
            vm((NY, words, blk // 4), BF),
            vm((8, NY, 32, blk // 4), BF),
            vm((7, NY, 32, blk // 4), BF),
            vm((NY, 32, blk // 4), BF),
            vm((3, 32, blk // 4), BF),
            vm((2, 8, 32, blk // 2), BF),
            vm((2, 7, 32, blk // 2), BF),
            vm((2, 8, 32, blk), BF),
            vm((2, 7, 32, blk), BF),
            vm((2, 32, blk), BF),
            vm((2, 2, 32, blk), BF),
            vm((STEPS, 4, NT, 16, cols), BF),
            vm((2, NT, 4, 16, rows // 2), F32),
            vm((2, NT, 4, 16, rows // 2), BF),
            vm((2, NT, 4, 16, rows // 2), BF),
            vm((2, NT, 4, 16, rows // 2), BF),
            vm((2, NT, NX * NC, 16, rows // 2), BF),
            vm((NT, 4, 16, rows), F32),
            vm((2, NX * NC, 16, rows), F32),
            dma((11,)),
            pltpu.SemaphoreType.REGULAR((4,)),
            dma((3,)), dma((3,)),
            dma((1,)), dma((1,)),
            dma((1,)), dma((1,)),
            dma((2,)), dma((2,)),
            dma((2,)), dma((2,)),
            dma((2,)), dma((2,)),
            dma((2,)), dma((2, 2)),
            dma((1,)), dma((1,)),
            dma((3, NT)), dma((3, NT)),
            dma((2, NT)), dma((2, NT)),
            dma((2, NT)), dma((2, NT)),
            dma((2, NT)), dma((2, NT)),
            dma((NT,)), dma((2,)),
        ],
        compiler_params=pltpu.CompilerParams(
            collective_id=0, has_side_effects=True, vmem_limit_bytes=30 * 1024 * 1024
        ),
        name="window",
    )(*(pltpu.with_memory_space_constraint(a, pltpu.HBM) for a in args))


def solution(mesh):
    in_specs = (P("src", "dst"), P("src", "dst"), P(None, None, "src"), P(None, "dst"), P(), P())
    out_specs = (P("src", "dst"), P("dst", "src"))
    return jax.shard_map(
        per_device, mesh=mesh, in_specs=in_specs, out_specs=out_specs, check_vma=False
    )
```

```python
import jax
import jax.numpy as jnp
from jax import lax
from jax.experimental import pallas as pl
from jax.experimental.pallas import tpu as pltpu
from jax.sharding import PartitionSpec as P

MESH = pl.DeviceIdType.MESH
NX, NY, NZ, NC = 4, 4, 8, 2
B = 256
STEPS = 3
NT = 4
SPLIT = (0, 3)
BF = jnp.bfloat16
F32 = jnp.float32
FAR = (4, 3, 5, 2, 6, 1, 7)
NEAR = (1, 7, 2, 6, 3, 5, 4)


def dev(x, y, z, c):
    return (y * NZ + z, x * NC + c)


def kernel(
    trans, emis, forw, beta, scales_in, tokens_in,
    counts, first,
    scales, tokens, tv, tt, ev, fv, bv, ft, sc, hot, eb, xb, rzb, sb, ryb,
    x2, rz2, x10, rz10, em_s, em,
    w, own, pb, pr, qb, orx, fp, fx,
    l_sem, rdy,
    e_s, e_r, zb_s, zb_r, yb_s, yb_r, z2_s, z2_r, zw_s, zw_r, z10_s, z10_r, pm_s, pm_r,
    ya_s, ya_r, y_s, y_r, pp_s, pp_r, o_s, o_r, zz_s, zz_r, fx_s, fx_r, ls_s, ls_r,
):
    s = lax.axis_index("src")
    d = lax.axis_index("dst")
    y, z = s // NZ, s % NZ
    x, c = d // NC, d % NC
    sib = 1 - c
    words = emis.shape[0]
    cols = emis.shape[1]
    blk = cols // 4
    hb = blk // 2
    qb_ = blk // 4
    rows = trans.shape[0]
    yo = pl.multiple_of(y * blk, blk)
    oc = z // 4
    q = z % 4
    qo = pl.multiple_of(q * blk, blk)
    qo_late = pl.multiple_of(q * blk + hb, hb)
    is_owner = c == oc

    def zp(i):
        return lax.rem(z + i, NZ)

    def yp(i):
        return lax.rem(y + i, NY)

    def xp(i):
        return lax.rem(x + i, NX)

    barrier = pltpu.get_barrier_semaphore()
    z_near = [dev(x, y, zp(i), c) for i in (1, NZ - 1)]
    x_near = [dev(xp(i), y, z, c) for i in (1, NX - 1)]
    peers = [dev(x, y, z, sib)] + [dev(x, yp(i), z, c) for i in range(1, NY)] + z_near + x_near

    def greet(sem, to):
        for p in to:
            pl.semaphore_signal(sem, inc=1, device_id=p, device_id_type=MESH)

    greet(barrier, peers)
    loads = [
        pltpu.make_async_copy(emis.at[:, pl.ds(yo, hb)], ev.at[0, y], l_sem.at[0]),
        pltpu.make_async_copy(
            emis.at[:, pl.ds(pl.multiple_of(y * blk + hb, hb), hb)], ev.at[1, y], l_sem.at[1]
        ),
        pltpu.make_async_copy(
            beta.at[pl.ds(pl.multiple_of(z * 32, 32), 32), pl.ds(yo, blk)], bv, l_sem.at[2]
        ),
        pltpu.make_async_copy(trans, tv, l_sem.at[3]),
        pltpu.make_async_copy(forw, fv, l_sem.at[4]),
        pltpu.make_async_copy(scales_in, scales, l_sem.at[5]),
        pltpu.make_async_copy(tokens_in, tokens, l_sem.at[6]),
    ]
    corner = [
        pltpu.make_async_copy(
            emis.at[:, j * blk + hb + qb_ : (j + 1) * blk], eb.at[j], l_sem.at[7 + j]
        )
        for j in range(NY)
    ]
    for cp in loads[-1:] + corner + loads[:-1]:
        cp.start()
    pl.semaphore_wait(barrier, len(peers))

    sent = []

    def send(src, dst, ss, rs, to, cond=None):
        cp = pltpu.make_async_remote_copy(
            src_ref=src, dst_ref=dst, send_sem=ss, recv_sem=rs, device_id=to, device_id_type=MESH
        )
        if cond is None:
            cp.start()
        else:
            pl.when(cond)(cp.start)

    def sent_all(size, sem, cond=None):
        sent.append((cond, size, sem))

    here = dev(x, y, z, sib)

    def whole(size, sem):
        return pltpu.make_async_remote_copy(
            src_ref=size, dst_ref=size, send_sem=sem, recv_sem=sem,
            device_id=here, device_id_type=MESH,
        )

    def arrive(size, sem, cond=None):
        wait = whole(size, sem).wait_recv
        if cond is None:
            wait()
        else:
            pl.when(cond)(wait)

    for h, lo, at, size in ((0, 0, 0, hb), (1, hb, 0, qb_), (2, hb + qb_, qb_, qb_)):
        dst = ev.at[min(h, 1), y, :, at : at + size]
        for i in (2, 1, 3):
            yt = yp(i)
            send(
                emis.at[:, pl.ds(pl.multiple_of(yt * blk + lo, qb_), size)],
                dst, e_s.at[h], e_r.at[h], dev(x, yt, z, c),
            )
        sent_all(ev.at[0, 0:3, :, 0:size], e_s.at[h])

    eye = lax.broadcasted_iota(jnp.int32, (B, B), 0) == lax.broadcasted_iota(jnp.int32, (B, B), 1)

    def as_column(row):
        col = jnp.sum(jnp.where(eye, jnp.broadcast_to(row, (B, B)), 0.0), axis=1, keepdims=True)
        return jnp.broadcast_to(col, (B, 128))

    def hot_rows(k):
        tok = as_column(tokens[k : k + 1, :].astype(F32))
        for j in range(NY):
            base = ((j * NZ + z) * words).astype(F32)
            for t in range(words // 128):
                lane = lax.broadcasted_iota(jnp.int32, (B, 128), 1).astype(F32) + (base + 128.0 * t)
                at = j * words + t * 128
                hot[k, :, at : at + 128] = jnp.where(tok == lane, 1.0, 0.0).astype(BF)

    def greet_ring(j):
        greet(rdy.at[j], z_near)

    def greeted_ring(j):
        pl.semaphore_wait(rdy.at[j], 2)

    greet_ring(0)
    greet(rdy.at[3], x_near)
    loads[6].wait()
    hot_rows(2)
    for cp in corner:
        cp.wait()
    mine_hot = hot[2, :, pl.ds(pl.multiple_of(y * words, words), words)]
    for j in range(NY):
        if j in (0, 2):
            greeted_ring(j // 2)
            greet_ring(j // 2 + 1)
        xb[:, j] = (
            jnp.dot(mine_hot, eb[j], preferred_element_type=F32).astype(BF).reshape(8, 32, qb_)
        )
    greeted_ring(2)
    for i in FAR:
        send(xb.at[zp(i)], rzb.at[i - 1], zb_s.at[0], zb_r.at[0], dev(x, y, zp(i), c))
    sent_all(rzb, zb_s.at[0])

    for k in (1, 0):
        hot_rows(k)
    for cp in loads[2:6]:
        cp.wait()
    sc[2] = as_column(scales[2:3, :]).reshape(16, 16, 128)
    pl.semaphore_wait(rdy.at[3], 2)

    def lookup(k, h, size):
        return jnp.dot(
            hot[k], ev[h, :, :, 0:size].reshape(NY * words, size), preferred_element_type=F32
        ).astype(BF).reshape(8, 32, size)

    for h, size in ((0, hb), (1, qb_)):
        loads[h].wait()
        arrive(ev.at[0, 0:3, :, 0:size], e_r.at[h])
        x2[h, :, :, 0:size] = lookup(2, h, size)
        for i in FAR:
            send(
                x2.at[h, zp(i), :, 0:size], rz2.at[h, i - 1, :, 0:size], z2_s.at[h], z2_r.at[h],
                dev(x, y, zp(i), c),
            )
        sent_all(rz2.at[h, :, :, 0:size], z2_s.at[h])
        part = pl.multiple_of((sib if h == 0 else c) * (rows // 2), rows // 2)
        for lo in range(0, cols, 512):
            tt[h, lo : lo + 512, :] = tv[pl.ds(part, rows // 2), lo : lo + 512].astype(F32).T.astype(BF)
    arrive(rzb, zb_r.at[0])
    tot = xb[z].astype(F32)
    for i in range(7):
        tot = tot + rzb[i].astype(F32)
    sb[...] = tot.astype(BF)
    for i in (2, 1, 3):
        send(sb.at[yp(i)], ryb.at[i - 1], yb_s.at[0], yb_r.at[0], dev(x, yp(i), z, c))
    sent_all(ryb, yb_s.at[0])
    arrive(ev.at[0, 0:3, :, 0:qb_], e_r.at[2])
    for kk in (1, 0):
        for h in range(2):
            x10[kk, :, :, h * hb : (h + 1) * hb] = lookup(kk, h, hb)

    def scaled(value, k, g):
        den = sc[k, g]
        return value / jnp.concatenate([den] * (value.shape[-1] // 128), axis=1)

    for h in range(2):
        size = (hb, qb_)[h]
        tot = x2[h, z, :, 0:size].astype(F32)
        arrive(rz2.at[h, :, :, 0:size], z2_r.at[h])
        for i in NEAR:
            tot = tot + rz2[h, i - 1, :, 0:size].astype(F32)
        if h == 1:
            arrive(ryb, yb_r.at[0])
            rest = sb[y].astype(F32)
            for i in range(3):
                rest = rest + ryb[i].astype(F32)
            tot = jnp.concatenate([tot, rest], axis=1)
        tot = tot * bv[:, h * hb : (h + 1) * hb].astype(F32)
        ho = pl.ds(pl.multiple_of(y * blk + h * hb, hb), hb)
        for u in range(2):
            w[2, z // 2, 2 * (z % 2) + u, :, ho] = scaled(
                tot[u * 16 : (u + 1) * 16], 2, 2 * z + u
            ).astype(BF)
        mine = w.at[2, z // 2, pl.ds(2 * (z % 2), 2), :, ho]
        for i in FAR:
            send(mine, mine, zw_s.at[h], zw_r.at[h], dev(x, y, zp(i), c))
        sent_all(rz2.at[h], zw_s.at[h])

    def spread(kk):
        for i in FAR:
            send(
                x10.at[kk, zp(i)], rz10.at[kk, i - 1], z10_s.at[kk], z10_r.at[kk],
                dev(x, y, zp(i), c),
            )
        sent_all(rz10.at[kk], z10_s.at[kk])

    spread(1)
    three_a = w.at[2, 0:3, :, :, 0 : 4 * hb]
    for h in range(2):
        ho = pl.ds(pl.multiple_of(y * blk + h * hb, hb), hb)
        arrive(rz2.at[h], zw_r.at[h])
        if h == 0:
            part = w.at[2, :, :, :, ho]
            for i in (2, 1, 3):
                send(part, part, ya_s.at[0], ya_r.at[0], dev(x, yp(i), z, c))
            sent_all(three_a, ya_s.at[0])
    def y_part(k, t, yt):
        if k == 2:
            return w.at[2, :, t, :, pl.ds(pl.multiple_of(yt * blk + hb, hb), hb)]
        return w.at[k, yt, t]

    def y_three(k, t):
        return w.at[k, 0:3, t, :, 0 : 4 * hb] if k == 2 or (k, t) == SPLIT else w.at[k, 0:3, t]

    def y_send(k, t):
        part = y_part(k, t, y)
        for i in (2, 1, 3):
            send(part, part, y_s.at[k, t], y_r.at[k, t], dev(x, yp(i), z, c))
        sent_all(y_three(k, t), y_s.at[k, t])

    for t in range(NT):
        y_send(2, t)
    spread(0)
    for k in (1, 0):
        sc[k] = as_column(scales[k : k + 1, :]).reshape(16, 16, 128)
    for k in range(STEPS):
        ft[:, k * B : (k + 1) * B] = fv[k].astype(F32).T.astype(BF)

    def wait_rows(k, t):
        if k == 2 and t == 0:
            arrive(three_a, ya_r.at[0])
        arrive(y_three(k, t), y_r.at[k, t])
        if (k, t) == SPLIT:
            arrive(w.at[k, 0:3, t, :, 0 : 4 * hb], ls_r.at[1], is_owner)
            arrive(w.at[k, :, t, :, 0 : 4 * hb], ls_r.at[1], jnp.logical_not(is_owner))

    def product(k, t, j):
        return jnp.dot(
            w[k, :, t].reshape(B // NT, cols), tt[j], preferred_element_type=F32
        ).reshape(4, 16, rows // 2)

    own_part = (x == y) & is_owner

    def partial_sums(k, t):
        wait_rows(k + 1, t)
        theirs, ours = product(k + 1, t, 0), product(k + 1, t, 1)
        pb[k, t] = theirs.astype(BF)
        own[k, t] = ours
        send(pb.at[k, t], pr.at[k, t], pp_s.at[k, t], pp_r.at[k, t], dev(x, y, z, sib))
        sent_all(pb.at[k, t], pp_s.at[k, t])

    def pair_sums(k, t):
        arrive(pr.at[k, t], pp_r.at[k, t])
        qb[k, t] = (own[k, t] + pr[k, t].astype(F32)).astype(BF)
        for r in range(NY):
            self_r = (x == y) & (y == r) & is_owner
            send(
                qb.at[k, t, r], orx.at[k, t, x * 2 + c], o_s.at[k, t], o_r.at[k, t],
                dev(y, r, z, oc), jnp.logical_not(self_r),
            )

            @pl.when(self_r)
            def _():
                orx[k, t, x * 2 + c] = qb[k, t, r]

        sent_all(qb.at[k, t, 0:3], o_s.at[k, t], own_part)
        sent_all(qb.at[k, t], o_s.at[k, t], jnp.logical_not(own_part))

    pm_self = (y == z // 2) & (z == 4 * c + y)

    def tiles(kk):
        acc = x10[kk, z].astype(F32)
        arrive(rz10.at[kk], z10_r.at[kk])
        for i in NEAR:
            acc = acc + rz10[kk, i - 1].astype(F32)
        em_s[kk] = acc.astype(BF)
        send(
            em_s.at[kk], em.at[kk, z % 2], pm_s.at[kk], pm_r.at[kk, z % 2],
            dev(x, z // 2, 4 * c + y, c), jnp.logical_not(pm_self),
        )
        sent_all(em_s.at[kk], pm_s.at[kk], jnp.logical_not(pm_self))

        @pl.when(pm_self)
        def _():
            em[kk, z % 2] = em_s[kk]

    def tiles_done(kk):
        for h in range(2):
            from_self = (y == q) & (z == 2 * y + h)
            arrive(em.at[kk, h], pm_r.at[kk, h], is_owner & jnp.logical_not(from_self))

    def owner(k, t):
        arrive(orx.at[k, t, 0:7], o_r.at[k, t], own_part)
        arrive(orx.at[k, t], o_r.at[k, t], is_owner & jnp.logical_not(own_part))

        @pl.when(is_owner)
        def _():
            halves = []
            for cc in range(2):
                acc = orx[k, t, cc].astype(F32)
                for xx in range(1, NX):
                    acc = acc + orx[k, t, 2 * xx + cc].astype(F32)
                halves.append(acc)
            msg = jnp.concatenate(halves, axis=1).astype(BF).astype(F32)
            lo = 16 * (t % 2)
            w[k, y, t, :, pl.ds(qo, blk)] = scaled(
                em[k, t // 2, lo : lo + 16].astype(F32) * msg, k, 4 * y + t
            ).astype(BF)

        if (k, t) == SPLIT:
            tile = w.at[k, y, t, :, pl.ds(qo, hb)]
            other = w.at[k, y, t, :, pl.ds(qo_late, hb)]
            for i in (2, 1, 3):
                send(other, other, ls_s.at[0], ls_r.at[0], dev(x, yp(i), z, c), is_owner)
            sent_all(w.at[k, 0, t, :, 0 : 3 * hb], ls_s.at[0], is_owner)
            for i in FAR:
                send(tile, tile, zz_s.at[k, t], zz_r.at[k, t], dev(x, y, zp(i), c), is_owner)
            sent_all(rz2.at[0, :, :, 0:qb_], zz_s.at[k, t], is_owner)
            return
        tile = w.at[k, y, t, :, pl.ds(qo, blk)]
        for i in FAR:
            send(tile, tile, zz_s.at[k, t], zz_r.at[k, t], dev(x, y, zp(i), c), is_owner)
        sent_all(rz2.at[0], zz_s.at[k, t], is_owner)

    def across(k, t):
        arrive(w.at[k, 0, t, :, 0 : 3 * hb], ls_r.at[0], is_owner)
        part = w.at[k, :, t, :, pl.ds(qo_late, hb)]
        for i in FAR:
            send(part, part, ls_s.at[1], ls_r.at[1], dev(x, y, zp(i), c), is_owner)
        sent_all(rz10.at[0], ls_s.at[1], is_owner)

    def column(k, t):
        if (k, t) == SPLIT:
            arrive(w.at[k, y, t, :, 0 : 3 * hb], zz_r.at[k, t], is_owner)
            arrive(w.at[k, y, t, :, 0 : 4 * hb], zz_r.at[k, t], jnp.logical_not(is_owner))
            for j in range(4):
                part = w.at[k, y, t, :, j * blk : j * blk + hb]
                for i in (2, 1, 3):
                    send(part, part, y_s.at[k, t], y_r.at[k, t], dev(x, yp(i), z, c))
            sent_all(y_three(k, t), y_s.at[k, t])
            return
        arrive(w.at[k, y, t, :, 0 : 3 * blk], zz_r.at[k, t], is_owner)
        arrive(w.at[k, y, t], zz_r.at[k, t], jnp.logical_not(is_owner))
        y_send(k, t)

    def last(t):
        wait_rows(0, t)
        for j, half in ((0, sib), (1, c)):
            fp[t, :, :, pl.ds(pl.multiple_of(half * (rows // 2), rows // 2), rows // 2)] = product(
                0, t, j
            )
        to = t // 2
        u = t % 2
        for i in (2, 1, 3, 0):
            send(
                fp.at[t, xp(i)], fx.at[u, 2 * i + c], fx_s.at[t], fx_r.at[u],
                dev(xp(i), y, z, to), c != to if i == 0 else None,
            )
        sent_all(fp.at[t], fx_s.at[t], c != to)
        sent_all(fp.at[t, 0:3], fx_s.at[t], c == to)

    partial_sums(1, 0)
    tiles(1)
    pair_sums(1, 0)
    partial_sums(1, 1)
    partial_sums(1, 2)
    pair_sums(1, 1)
    partial_sums(1, 3)
    pair_sums(1, 2)
    pair_sums(1, 3)
    tiles_done(1)
    owner(1, 0)
    owner(1, 1)
    owner(1, 2)
    column(1, 0)
    owner(1, 3)
    column(1, 1)
    tiles(0)
    column(1, 2)
    partial_sums(0, 0)
    pair_sums(0, 0)
    column(1, 3)
    partial_sums(0, 1)
    pair_sums(0, 1)
    partial_sums(0, 2)
    pair_sums(0, 2)
    tiles_done(0)
    owner(0, 0)
    partial_sums(0, 3)
    pair_sums(0, 3)
    owner(0, 1)
    owner(0, 2)
    column(0, 0)
    owner(0, 3)
    column(0, 1)
    column(0, 2)
    last(0)
    across(0, 3)
    column(0, 3)
    last(1)
    last(2)
    last(3)

    def count_block(n):
        lo = n * 256
        acc = jnp.dot(
            ft[...], w[:, :, :, :, lo : lo + 256].reshape(STEPS * B, 256), preferred_element_type=F32
        )
        counts[:, lo : lo + 256] = tv[:, lo : lo + 256].astype(F32) * acc * (32.0 / (STEPS * B))

    for n in range(cols // 256):
        count_block(n)
    for u in range(2):
        tot = fp[2 * c + u, x]
        arrive(fx.at[u, 0:7], fx_r.at[u])
        for j in [sib] + list(range(2, 8)):
            tot = tot + fx[u, j]
        first[u * 16 : (u + 1) * 16] = tot
    for cond, size, sem in sent:
        wait = whole(size, sem).wait_send
        if cond is None:
            wait()
        else:
            pl.when(cond)(wait)


def per_device(*args):
    transition, emission = args[:2]
    rows, cols = transition.shape
    blk = cols // 4
    words = emission.shape[0]
    dma = pltpu.SemaphoreType.DMA
    vm = pltpu.VMEM
    hbm = pl.BlockSpec(memory_space=pltpu.HBM)
    vmem = pl.BlockSpec(memory_space=pltpu.VMEM)
    return pl.pallas_call(
        kernel,
        out_shape=(
            jax.ShapeDtypeStruct((rows, cols), F32),
            jax.ShapeDtypeStruct((B // 8, rows), F32),
        ),
        in_specs=[hbm] * 6,
        out_specs=(vmem, vmem),
        scratch_shapes=[
            vm((STEPS, B), F32),
            vm((STEPS, B), jnp.int32),
            vm((rows, cols), BF),
            vm((2, cols, rows // 2), BF),
            vm((2, NY, words, blk // 2), BF),
            vm((STEPS, B, rows), BF),
            vm((32, blk), BF),
            vm((rows, STEPS * B), BF),
            vm((STEPS, 16, 16, 128), F32),
            vm((STEPS, B, NY * words), BF),
            vm((NY, words, blk // 4), BF),
            vm((8, NY, 32, blk // 4), BF),
            vm((7, NY, 32, blk // 4), BF),
            vm((NY, 32, blk // 4), BF),
            vm((3, 32, blk // 4), BF),
            vm((2, 8, 32, blk // 2), BF),
            vm((2, 7, 32, blk // 2), BF),
            vm((2, 8, 32, blk), BF),
            vm((2, 7, 32, blk), BF),
            vm((2, 32, blk), BF),
            vm((2, 2, 32, blk), BF),
            vm((STEPS, 4, NT, 16, cols), BF),
            vm((2, NT, 4, 16, rows // 2), F32),
            vm((2, NT, 4, 16, rows // 2), BF),
            vm((2, NT, 4, 16, rows // 2), BF),
            vm((2, NT, 4, 16, rows // 2), BF),
            vm((2, NT, NX * NC, 16, rows // 2), BF),
            vm((NT, 4, 16, rows), F32),
            vm((2, NX * NC, 16, rows), F32),
            dma((11,)),
            pltpu.SemaphoreType.REGULAR((4,)),
            dma((3,)), dma((3,)),
            dma((1,)), dma((1,)),
            dma((1,)), dma((1,)),
            dma((2,)), dma((2,)),
            dma((2,)), dma((2,)),
            dma((2,)), dma((2,)),
            dma((2,)), dma((2, 2)),
            dma((1,)), dma((1,)),
            dma((3, NT)), dma((3, NT)),
            dma((2, NT)), dma((2, NT)),
            dma((2, NT)), dma((2, NT)),
            dma((2, NT)), dma((2, NT)),
            dma((NT,)), dma((2,)),
            dma((2,)), dma((2,)),
        ],
        compiler_params=pltpu.CompilerParams(
            collective_id=0, has_side_effects=True, vmem_limit_bytes=30 * 1024 * 1024
        ),
        name="window",
    )(*(pltpu.with_memory_space_constraint(a, pltpu.HBM) for a in args))


def solution(mesh):
    in_specs = (P("src", "dst"), P("src", "dst"), P(None, None, "src"), P(None, "dst"), P(), P())
    out_specs = (P("src", "dst"), P("dst", "src"))
    return jax.shard_map(
        per_device, mesh=mesh, in_specs=in_specs, out_specs=out_specs, check_vma=False
    )
```
